512 devices in a mesh: gx: 8 (over y, core), gy: 4 (over z_lo), gz: 16 (over z_hi, x).
Axes of the slice: x: 4, y: 4, z: 16 (z_hi: 4, z_lo: 4; z = z_hi * 4 + z_lo), core: 2. Of those that a mesh axis runs over, the one named last changes fastest.
Arguments:
- source: bfloat16 [32, 96, 8192], P('gx', 'gy', 'gz'), may hold values from -6 to 6
- tangent: bfloat16 [32, 96, 8192], P('gx', 'gy', 'gz'), may hold values from -6 to 6
- first_weight: bfloat16 [3, 3, 3, 64, 64], replicated, may hold values from -0.15625 to 0.15625
- first_bias: float32 [64], replicated, may hold values from -3 to 3
- second_weight: bfloat16 [3, 3, 3, 64, 64], replicated, may hold values from -0.15625 to 0.15625
- second_bias: float32 [64], replicated, may hold values from -3 to 3
Outputs:
- result: bfloat16 [32, 96, 8192], P('gx', 'gy', 'gz')
- result_tangent: bfloat16 [32, 96, 8192], P('gx', 'gy', 'gz')
The draws below stay inside these ranges and needn't reach their ends.
All inputs are finite; a program needn't handle non-finite values.
Results may differ from the reference program's by a relative error of at most 0.0052.
Values may be sent and summed in bfloat16 or wider, within the bound.
No kernel may reach another device: no remote copies, remote signals or barrier semaphores. Data moves between devices by JAX's collectives and lax.ppermute only.
A program may use at most 64 MiB of HBM per device.

```python
import jax
import jax.numpy as jnp
from jax import lax

C = 64
NX = 32
NY = 96
NZ = 128


def level_of(rng, extent, shards, smallest, top_value):
    def one(dim, parts):
        draws = jax.random.uniform(jax.random.fold_in(jax.random.fold_in(rng, 6), dim), (parts,), jnp.float32, smallest / len(shards), top_value / len(shards))
        return jnp.repeat(jnp.exp(draws), extent[dim] // parts).reshape((-1,) + (1,) * (len(extent) - dim - 1))

    loudness = one(*shards[0])
    for cut in shards[1:]:
        loudness = loudness * one(*cut)
    return loudness


def bell_draw(key, extent, scale, most, pieces=(), kind=jnp.bfloat16):
    values = jax.random.normal(key, extent, jnp.float32) * scale
    if len(pieces) > 0:
        values = level_of(key, extent, pieces, -0.22, 0.18) * values
    return jnp.clip(values, min=-most, max=most).astype(kind)


def setup_inputs(seed: int = 0) -> dict:
    splits = jax.random.split(jax.random.key(seed), 7)
    return {
        "source": bell_draw(splits[0], (NX, NY, NZ * C), 1.0, 6.0, ((0, 8), (1, 4), (2, 16))),
        "tangent": bell_draw(splits[1], (NX, NY, NZ * C), 1.0, 6.0, ((0, 8), (1, 4), (2, 16))),
        "first_weight": bell_draw(splits[2], (3, 3, 3, C, C), (27 * C) ** -0.5, 0.15625),
        "first_bias": bell_draw(splits[3], (C,), 0.5, 3.0, (), jnp.float32),
        "second_weight": bell_draw(splits[4], (3, 3, 3, C, C), (27 * C) ** -0.5, 0.15625),
        "second_bias": bell_draw(splits[5], (C,), 0.5, 3.0, (), jnp.float32),
    }


def convolve(field, weight):
    return lax.conv_general_dilated(field, weight.astype(jnp.float32), (1, 1, 1), "SAME", dimension_numbers=("NDHWC", "DHWIO", "NDHWC"), precision=lax.Precision.HIGHEST)


def silu_slope(pre):
    sig = jax.nn.sigmoid(pre)
    return sig * (1.0 + pre * (1.0 - sig))


def reference(source, tangent, first_weight, first_bias, second_weight, second_bias):
    shape5 = (2, NX, NY, NZ, C)
    both = jnp.stack([source, tangent]).astype(jnp.float32).reshape(shape5)
    out1 = convolve(both, first_weight)
    pre1 = out1[0] + first_bias
    hidden = jax.nn.silu(pre1).astype(jnp.bfloat16)
    hidden_tangent = (silu_slope(pre1) * out1[1]).astype(jnp.bfloat16)
    both2 = jnp.stack([hidden, hidden_tangent]).astype(jnp.float32)
    out2 = convolve(both2, second_weight)
    pre2 = out2[0] + second_bias
    result = jax.nn.silu(pre2).astype(jnp.bfloat16).reshape(NX, NY, NZ * C)
    result_tangent = (silu_slope(pre2) * out2[1]).astype(jnp.bfloat16).reshape(NX, NY, NZ * C)
    return result, result_tangent
```

```python
import functools

import jax
import jax.numpy as jnp
from jax import lax
from jax.experimental import pallas as pl
from jax.experimental.pallas import tpu as pltpu
from jax.sharding import PartitionSpec as P

F32 = jnp.float32
BF16 = jnp.bfloat16


def swap(axis, head, tail):
    count = lax.axis_size(axis)
    even = lax.axis_index(axis) % 2 == 0
    far = [(i, i + 1) for i in range(1, count - 1, 2)]
    near = [(i, i + 1) for i in range(0, count - 1, 2)]
    both = lambda pairs: pairs + [(j, i) for i, j in pairs]
    got_far = lax.ppermute(jnp.where(even, head, tail), axis, both(far))
    got_near = lax.ppermute(jnp.where(even, tail, head), axis, both(near))
    return got_far, got_near


def sides(axis, far, near):
    even = lax.axis_index(axis) % 2 == 0
    return jnp.where(even, far, near), jnp.where(even, near, far)


def weight_kernel(first, second, bias_a, bias_b, out_a, out_b, bias_out):
    for source, target in ((first, out_a), (second, out_b)):
        target[...] = jnp.zeros(target.shape, BF16)
        for dy in range(3):
            for dx in range(3):
                w = source[dx, dy]
                for k in range(2):
                    base = (dy * 4 + dx + k) * 256
                    target[base : base + 192, 128 * k : 128 * k + 64] = w
                    target[base + 64 : base + 256, 128 * k + 64 : 128 * k + 128] = w
    for row, bias in enumerate((bias_a, bias_b)):
        b = bias[...]
        bias_out[row : row + 1, :] = jnp.concatenate([b, b, b, b], axis=1)


def silu_pair(pre, direction):
    sig = jax.nn.sigmoid(pre)
    return pre * sig, sig * (1.0 + pre * (1.0 - sig)) * direction


def layer(shifted, weights, bias, planes, pairs, rows):
    parts = []
    for f in range(2):
        for xp in range(planes // 2):
            for p in range(pairs):
                parts.append(
                    jnp.concatenate(
                        [
                            shifted[dy, f, 2 * xp + j, :, 128 * p : 128 * p + 256]
                            for dy in range(3)
                            for j in range(4)
                        ],
                        axis=1,
                    )
                )
    acc = jnp.dot(jnp.concatenate(parts, axis=0), weights[...], preferred_element_type=F32)
    half = acc.shape[0] // 2
    return silu_pair(acc[:half] + bias, acc[half:])


def conv_kernel(
    place, src, tan, zf, zn, xf, xn, yf, yn, wa, wb, bias, out, out_t, ext, sh1, hid, sh2
):
    nx, ny, nz = src.shape
    pairs = nz // 128

    def pick(axis, far, near):
        even = place[3 + axis] == 1
        a, b = far[...], near[...]
        return jnp.where(even, a, b).astype(F32), jnp.where(even, b, a).astype(F32)

    zl, zr = pick(2, zf, zn)
    xl, xr = pick(0, xf, xn)
    yl, yr = pick(1, yf, yn)
    own_y = slice(2, 2 + ny)
    for f, field in enumerate((src, tan)):
        ext[f, 2 : 2 + nx, own_y, 128 : 128 + nz] = field[...].astype(F32)
    ext[:, 2 : 2 + nx, own_y, 0:128] = zl
    ext[:, 2 : 2 + nx, own_y, 128 + nz :] = zr
    ext[:, 0:2, own_y, :] = xl
    ext[:, 2 + nx :, own_y, :] = xr
    ext[:, :, 0:2, :] = yl
    ext[:, :, 2 + ny : 4 + ny, :] = yr
    rows = sh1.shape[3]
    for dy in range(3):
        sh1[dy] = ext[:, :, dy : dy + rows, :].astype(BF16)

    h, ht = layer(sh1, wa, bias[0:1, :], nx + 2, pairs + 1, rows)
    for f, value in enumerate((h, ht)):
        at = 0
        for xp in range((nx + 2) // 2):
            for p in range(pairs + 1):
                for k in range(2):
                    hid[f, 2 * xp + k, 0:rows, 128 * p : 128 * p + 128] = value[
                        at : at + rows, 128 * k : 128 * k + 128
                    ]
                at += rows

    @pl.when(place[0] == 0)
    def _():
        hid[:, 0, :, :] = jnp.zeros_like(hid[:, 0, :, :])

    @pl.when(place[0] == place[6] - 1)
    def _():
        hid[:, nx + 1, :, :] = jnp.zeros_like(hid[:, nx + 1, :, :])

    @pl.when(place[1] == 0)
    def _():
        hid[:, :, 0:1, :] = jnp.zeros_like(hid[:, :, 0:1, :])

    @pl.when(place[1] == place[7] - 1)
    def _():
        hid[:, :, ny + 1 : ny + 2, :] = jnp.zeros_like(hid[:, :, ny + 1 : ny + 2, :])

    @pl.when(place[2] == 0)
    def _():
        hid[:, :, :, 0:64] = jnp.zeros_like(hid[:, :, :, 0:64])

    @pl.when(place[2] == place[8] - 1)
    def _():
        hid[:, :, :, nz + 64 :] = jnp.zeros_like(hid[:, :, :, nz + 64 :])

    for dy in range(3):
        sh2[dy] = hid[:, :, dy : dy + rows, :].astype(BF16)
    r, rt = layer(sh2, wb, bias[1:2, :], nx, pairs, rows)
    for target, value in ((out, r), (out_t, rt)):
        at = 0
        for xp in range(nx // 2):
            for p in range(pairs):
                for k in range(2):
                    target[2 * xp + k, :, 128 * p : 128 * p + 128] = value[
                        at : at + ny, 128 * k : 128 * k + 128
                    ].astype(BF16)
                at += rows


VM = pl.BlockSpec(memory_space=pltpu.VMEM)
SM = pl.BlockSpec(memory_space=pltpu.SMEM)


def shards(source, tangent, first_weight, first_bias, second_weight, second_bias):
    nx, ny, nz = source.shape
    own = jnp.stack([source, tangent])
    names = ("gx", "gy", "gz")
    index = [lax.axis_index(a) for a in names]
    place = jnp.stack(
        [i.astype(jnp.int32) for i in index]
        + [(i % 2 == 0).astype(jnp.int32) for i in index]
        + [jnp.int32(lax.axis_size(a)) for a in names]
    )
    wa, wb, bias = pl.pallas_call(
        weight_kernel,
        in_specs=[VM] * 4,
        out_specs=[VM] * 3,
        out_shape=[
            jax.ShapeDtypeStruct((3072, 256), BF16),
            jax.ShapeDtypeStruct((3072, 256), BF16),
            jax.ShapeDtypeStruct((2, 256), F32),
        ],
        compiler_params=pltpu.CompilerParams(vmem_limit_bytes=16 << 20),
        name="weights",
    )(
        first_weight.reshape(3, 3, 192, 64),
        second_weight.reshape(3, 3, 192, 64),
        first_bias.reshape(1, 64),
        second_bias.reshape(1, 64),
    )
    zf, zn = swap("gz", own[..., :128], own[..., nz - 128 :])
    zl, zr = sides("gz", zf, zn)
    ext = jnp.concatenate([zl, own, zr], axis=3)
    xf, xn = swap("gx", ext[:, :2], ext[:, nx - 2 :])
    xl, xr = sides("gx", xf, xn)
    ends = lambda at: jnp.concatenate(
        [part[:, :, at : at + 2] for part in (xl, ext, xr)], axis=1
    )
    yf, yn = swap("gy", ends(0), ends(ny - 2))
    rows = ny + 8
    shape = jax.ShapeDtypeStruct((nx, ny, nz), BF16)
    return tuple(
        pl.pallas_call(
            conv_kernel,
            in_specs=[SM] + [VM] * 11,
            out_specs=[VM] * 2,
            out_shape=[shape, shape],
            scratch_shapes=[
                pltpu.VMEM((2, nx + 4, rows + 8, nz + 256), F32),
                pltpu.VMEM((3, 2, nx + 4, rows, nz + 256), BF16),
                pltpu.VMEM((2, nx + 2, rows + 8, nz + 128), F32),
                pltpu.VMEM((3, 2, nx + 2, rows, nz + 128), BF16),
            ],
            compiler_params=pltpu.CompilerParams(vmem_limit_bytes=40 << 20),
            name="conv",
        )(place, source, tangent, zf, zn, xf, xn, yf, yn, wa, wb, bias)
    )


def solution(mesh):
    return jax.shard_map(
        shards,
        mesh=mesh,
        in_specs=(P("gx", "gy", "gz"), P("gx", "gy", "gz"), P(), P(), P(), P()),
        out_specs=(P("gx", "gy", "gz"), P("gx", "gy", "gz")),
        check_vma=False,
    )
```

```python
import jax
import jax.numpy as jnp
from jax import lax
from jax.experimental import pallas as pl
from jax.experimental.pallas import tpu as pltpu
from jax.sharding import PartitionSpec as P


F32 = jnp.float32
BF16 = jnp.bfloat16
ROWS = 32
VM = pl.BlockSpec(memory_space=pltpu.VMEM)
SM = pl.BlockSpec(memory_space=pltpu.SMEM)
HB = pl.BlockSpec(memory_space=pl.ANY)


def swap_pairs(axis, first):
    count = lax.axis_size(axis)
    pairs = [(i, i + 1) for i in range(first, count - 1, 2)]
    return pairs + [(j, i) for i, j in pairs]


def swap(axis, head, tail):
    even = lax.axis_index(axis) % 2 == 0
    to_far = jnp.where(even, head, tail)
    to_near = jnp.where(even, tail, head)
    far = lax.ppermute(to_far, axis, swap_pairs(axis, 1))
    near = lax.ppermute(to_near, axis, swap_pairs(axis, 0))
    return far, near


def sides(axis, far, near):
    even = lax.axis_index(axis) % 2 == 0
    return jnp.where(even, far, near), jnp.where(even, near, far)


def pick(even, far, near):
    a, b = far[...], near[...]
    return jnp.where(even, a, b).astype(F32), jnp.where(even, b, a).astype(F32)


def weight_kernel(first, second, bias_a, bias_b, out_a, out_b, bias_out, raw, sems):
    copies = [
        pltpu.make_async_copy(source, raw.at[n], sems.at[n])
        for n, source in enumerate((first, second))
    ]
    for copy in copies:
        copy.start()
    for row, bias in enumerate((bias_a, bias_b)):
        b = bias[...]
        bias_out[row : row + 1, :] = jnp.concatenate([b, b, b, b], axis=1)
    for n, target in enumerate((out_a, out_b)):
        target[...] = jnp.zeros(target.shape, BF16)
        copies[n].wait()
        for dy in range(3):
            for dx in range(3):
                w = raw[n, dx, dy]
                for k in range(2):
                    base = ((dx + k) * 3 + dy) * 256
                    target[base : base + 192, 128 * k : 128 * k + 64] = w
                    target[base + 64 : base + 256, 128 * k + 64 : 128 * k + 128] = w


def taps(read, starts, pairs):
    return jnp.concatenate(
        [
            jnp.concatenate(
                [read(dy, x, p) for x in planes for dy in range(3)], axis=1
            )
            for planes in starts
            for p in range(pairs)
        ],
        axis=0,
    )


def dot(lhs, rhs):
    return jnp.dot(lhs, rhs, preferred_element_type=F32)


def shift_rows(ext, shifted):
    for dy in range(3):
        for x in range(shifted.shape[1]):
            both = ext[:, x, dy : dy + ROWS, :].astype(BF16)
            shifted[dy, x] = both.reshape(2 * ROWS, both.shape[2])


def own_kernel(place, own, zf, zn, wa, acc, ext, shifted):
    nx, ny, nz = own.shape[1:]
    zl, zr = pick(place[5] == 1, zf, zn)
    ext[:, :, 0:2, :] = jnp.zeros_like(ext[:, :, 0:2, :])
    ext[:, :, 2 + ny :, :] = jnp.zeros_like(ext[:, :, 2 + ny :, :])
    ext[:, :, 2 : 2 + ny, 128 : 128 + nz] = own[...].astype(F32)
    ext[:, :, 2 : 2 + ny, 0:128] = zl
    ext[:, :, 2 : 2 + ny, 128 + nz :] = zr
    shift_rows(ext, shifted)
    read = lambda dy, x, p: shifted[dy, x, :, 128 * p : 128 * p + 256]
    pairs = nz // 128 + 1
    half = wa.shape[0] // 2
    size = pairs * 2 * ROWS
    last = nx // 2
    low = dot(taps(read, [(2 * i, 2 * i + 1) for i in range(last)], pairs), wa[:half])
    high = dot(taps(read, [(2 * i, 2 * i + 1) for i in range(last)], pairs), wa[half:])
    acc[0] = high[:size]
    for i in range(1, last):
        acc[i] = high[i * size : i * size + size] + low[(i - 1) * size : i * size]
    acc[last] = low[(last - 1) * size :]


def side_kernel(place, xf, xn, wa, acc, out, ext, shifted):
    ny = xf.shape[2]
    xl, xr = pick(place[3] == 1, xf, xn)
    ext[:, :, 0:2, :] = jnp.zeros_like(ext[:, :, 0:2, :])
    ext[:, :, 2 + ny :, :] = jnp.zeros_like(ext[:, :, 2 + ny :, :])
    ext[:, 0:2, 2 : 2 + ny, :] = xl
    ext[:, 2:4, 2 : 2 + ny, :] = xr
    shift_rows(ext, shifted)
    read = lambda dy, x, p: shifted[dy, x, :, 128 * p : 128 * p + 256]
    pairs = ext.shape[3] // 128 - 1
    half = wa.shape[0] // 2
    out[0] = acc[0] + dot(taps(read, [(0, 1)], pairs), wa[:half])
    out[1] = acc[acc.shape[0] - 1] + dot(taps(read, [(2, 3)], pairs), wa[half:])


def silu_pair(pre, direction):
    sig = jax.nn.sigmoid(pre)
    return pre * sig, sig * (1.0 + pre * (1.0 - sig)) * direction


def last_kernel(
    place, yf, yn, mid, ends, wa, wb, bias, out, out_t, edge, acc, hid, shifted
):
    nx, ny, nz = out.shape
    pairs = nz // 128
    half = wa.shape[0] // 2
    yl, yr = pick(place[4] == 1, yf, yn)
    edge[...] = jnp.zeros_like(edge)
    edge[0, :, :, 0:2, :] = yl
    edge[1, :, :, 0:1, :] = yl[:, :, 1:2]
    edge[1, :, :, 3:4, :] = yr[:, :, 0:1]
    edge[2, :, :, 2:4, :] = yr

    def read_edge(dy, x, p):
        part = edge[dy, :, x, :, 128 * p : 128 * p + 256]
        return part.reshape(16, 256).astype(BF16)

    blocks = nx // 2 + 1
    low = taps(read_edge, [(2 * i, 2 * i + 1) for i in range(blocks)], pairs + 1)
    high = taps(read_edge, [(2 * i + 2, 2 * i + 3) for i in range(blocks)], pairs + 1)
    extra = dot(low, wa[:half]) + dot(high, wa[half:])
    for i in range(blocks):
        if i == 0:
            acc[i] = ends[0]
        elif i == blocks - 1:
            acc[i] = ends[1]
        else:
            acc[i] = mid[i]
        for g in range(2 * (pairs + 1)):
            at = (i * 2 * (pairs + 1) + g) * 8
            top = ROWS * g
            low_end = top + ny
            acc[i, top : top + 2, :] += extra[at : at + 2]
            acc[i, low_end : low_end + 2, :] += extra[at + 2 : at + 4]
    b = bias[0:1, :]
    for i in range(blocks):
        for p in range(pairs + 1):
            at = p * 2 * ROWS
            value = silu_pair(
                acc[i, at : at + ROWS, :] + b, acc[i, at + ROWS : at + 2 * ROWS, :]
            )
            for f in range(2):
                for k in range(2):
                    hid[f, 2 * i + k, 0:ROWS, 128 * p : 128 * p + 128] = value[f][
                        :, 128 * k : 128 * k + 128
                    ]

    def clear(when, index):
        @pl.when(when)
        def _():
            hid[index] = jnp.zeros_like(hid[index])

    every = slice(None)
    clear(place[0] == 0, (every, 0))
    clear(place[0] == place[6] - 1, (every, nx + 1))
    clear(place[1] == 0, (every, every, slice(0, 1)))
    clear(place[1] == place[7] - 1, (every, every, slice(ny + 1, ny + 2)))
    clear(place[2] == 0, (every, every, every, slice(0, 64)))
    clear(place[2] == place[8] - 1, (every, every, every, slice(nz + 64, nz + 128)))

    for dy in range(3):
        for x in range(nx + 2):
            both = jnp.concatenate([hid[f, x, dy : dy + ny, :] for f in range(2)], axis=0)
            shifted[dy, x] = both.astype(BF16)
    read = lambda dy, x, p: shifted[dy, x, :, 128 * p : 128 * p + 256]
    blocks = nx // 2
    low = taps(read, [(2 * i, 2 * i + 1) for i in range(blocks)], pairs)
    high = taps(read, [(2 * i + 2, 2 * i + 3) for i in range(blocks)], pairs)
    total = dot(low, wb[:half]) + dot(high, wb[half:])
    b = bias[1:2, :]
    for i in range(blocks):
        for p in range(pairs):
            at = (i * pairs + p) * 2 * ny
            value = silu_pair(total[at : at + ny] + b, total[at + ny : at + 2 * ny])
            for target, part in zip((out, out_t), value):
                for k in range(2):
                    target[2 * i + k, :, 128 * p : 128 * p + 128] = part[
                        :, 128 * k : 128 * k + 128
                    ].astype(BF16)


def call(kernel, ins, outs, scratch, args, mib=24):
    return pl.pallas_call(
        kernel,
        in_specs=ins,
        out_specs=[VM] * len(outs),
        out_shape=[jax.ShapeDtypeStruct(*o) for o in outs],
        scratch_shapes=scratch,
        compiler_params=pltpu.CompilerParams(vmem_limit_bytes=mib << 20),
    )(*args)


def shards(source, tangent, first_weight, first_bias, second_weight, second_bias):
    nx, ny, nz = source.shape
    own = lax.optimization_barrier(jnp.stack([source, tangent]))
    names = ("gx", "gy", "gz")
    index = [lax.axis_index(a) for a in names]
    place = jnp.stack(
        [i.astype(jnp.int32) for i in index]
        + [(i % 2 == 0).astype(jnp.int32) for i in index]
        + [jnp.int32(lax.axis_size(a)) for a in names]
    )
    wa, wb, bias = call(
        weight_kernel,
        [HB, HB, VM, VM],
        [((3072, 256), BF16), ((3072, 256), BF16), ((2, 256), F32)],
        [pltpu.VMEM((2, 3, 3, 192, 64), BF16), pltpu.SemaphoreType.DMA((2,))],
        (
            first_weight.reshape(3, 3, 192, 64),
            second_weight.reshape(3, 3, 192, 64),
            first_bias.reshape(1, 64),
            second_bias.reshape(1, 64),
        ),
    )
    zf, zn = swap("gz", own[..., :128], own[..., nz - 128 :])
    zl, zr = sides("gz", zf, zn)
    ext = jnp.concatenate([zl, own, zr], axis=3)
    xf, xn = swap("gx", ext[:, :2], ext[:, nx - 2 :])
    xl, xr = sides("gx", xf, xn)
    ends = lambda at: jnp.concatenate(
        [part[:, :, at : at + 2] for part in (xl, ext, xr)], axis=1
    )
    yf, yn = swap("gy", ends(0), ends(ny - 2))

    wide = nz + 256
    blocks = nx // 2 + 1
    size = (nz // 128 + 1) * 2 * ROWS
    work = [
        pltpu.VMEM((2, 4, ROWS + 8, wide), F32),
        pltpu.VMEM((3, 4, 2 * ROWS, wide), BF16),
    ]
    (mid,) = call(
        own_kernel,
        [SM] + [VM] * 4,
        [((blocks, size, 256), F32)],
        [
            pltpu.VMEM((2, nx, ROWS + 8, wide), F32),
            pltpu.VMEM((3, nx, 2 * ROWS, wide), BF16),
        ],
        (place, own, zf, zn, wa),
    )
    (outer,) = call(
        side_kernel,
        [SM] + [VM] * 4,
        [((2, size, 256), F32)],
        work,
        (place, xf, xn, wa, mid),
    )
    block = ((nx, ny, nz), BF16)
    return tuple(
        call(
            last_kernel,
            [SM] + [VM] * 7,
            [block, block],
            [
                pltpu.VMEM((3, 2, nx + 4, 8, wide), F32),
                pltpu.VMEM((blocks, size, 256), F32),
                pltpu.VMEM((2, nx + 2, ROWS + 8, nz + 128), F32),
                pltpu.VMEM((3, nx + 2, 2 * ny, nz + 128), BF16),
            ],
            (place, yf, yn, mid, outer, wa, wb, bias),
        )
    )


def solution(mesh):
    return jax.shard_map(
        shards,
        mesh=mesh,
        in_specs=(P("gx", "gy", "gz"), P("gx", "gy", "gz"), P(), P(), P(), P()),
        out_specs=(P("gx", "gy", "gz"), P("gx", "gy", "gz")),
        check_vma=False,
    )
```

```python
import jax
import jax.numpy as jnp
from jax import lax
from jax.experimental import pallas as pl
from jax.experimental.pallas import tpu as pltpu
from jax.sharding import PartitionSpec as P


F32 = jnp.float32
BF16 = jnp.bfloat16
ROWS = 32
VM = pl.BlockSpec(memory_space=pltpu.VMEM)
SM = pl.BlockSpec(memory_space=pltpu.SMEM)
HB = pl.BlockSpec(memory_space=pltpu.HBM)


def swap_pairs(axis, first):
    count = lax.axis_size(axis)
    pairs = [(i, i + 1) for i in range(first, count - 1, 2)]
    return pairs + [(j, i) for i, j in pairs]


def swap(axis, head, tail):
    even = lax.axis_index(axis) % 2 == 0
    to_far = jnp.where(even, head, tail)
    to_near = jnp.where(even, tail, head)
    far = lax.ppermute(to_far, axis, swap_pairs(axis, 1))
    near = lax.ppermute(to_near, axis, swap_pairs(axis, 0))
    return far, near


def sides(axis, far, near):
    even = lax.axis_index(axis) % 2 == 0
    return jnp.where(even, far, near), jnp.where(even, near, far)


def pick(even, far, near):
    a, b = far[...], near[...]
    return jnp.where(even, a, b).astype(F32), jnp.where(even, b, a).astype(F32)


def weight_kernel(first, second, bias_a, bias_b, out_a, out_b, bias_out, raw, low, sems):
    copies = [
        pltpu.make_async_copy(source, target, sems.at[n])
        for n, (source, target) in enumerate(
            (
                (first, raw.at[0]),
                (second, raw.at[1]),
                (bias_a, low.at[0]),
                (bias_b, low.at[1]),
            )
        )
    ]
    for copy in copies:
        copy.start()
    gap = jnp.zeros((64, 64), BF16)
    for n, target in enumerate((out_a, out_b)):
        copies[n].wait()
        for tap in range(9):
            w = raw[n, tap]
            target[256 * tap : 256 * tap + 256, :] = jnp.concatenate(
                [
                    jnp.concatenate([w, gap], axis=0),
                    jnp.concatenate([gap, w], axis=0),
                ],
                axis=1,
            )
    for row in range(2):
        copies[2 + row].wait()
        b = low[row]
        bias_out[row : row + 1, :] = jnp.concatenate([b, b, b, b], axis=1)


def columns(weights, planes):
    none = jnp.zeros((256, 128), BF16)

    def tap(dx, dy):
        if not 0 <= dx <= 2:
            return none
        at = 256 * (3 * dx + dy)
        return weights[at : at + 256, :]

    return jnp.concatenate(
        [
            jnp.concatenate([tap(j, dy), tap(j - 1, dy)], axis=1)
            for j in planes
            for dy in range(3)
        ],
        axis=0,
    )


def taps(read, starts, pairs):
    return jnp.concatenate(
        [
            jnp.concatenate(
                [read(dy, x, p) for x in planes for dy in range(3)], axis=1
            )
            for planes in starts
            for p in range(pairs)
        ],
        axis=0,
    )


def dot(lhs, rhs):
    return jnp.dot(lhs, rhs, preferred_element_type=F32)


def shift_rows(ext, shifted):
    for dy in range(3):
        for x in range(shifted.shape[1]):
            both = ext[:, x, dy : dy + ROWS, :].astype(BF16)
            shifted[dy, x] = both.reshape(2 * ROWS, both.shape[2])


def own_kernel(place, own, zf, zn, wa, mid, ends, ext, shifted):
    nx, ny, nz = own.shape[1:]
    zl, zr = pick(place[5] == 1, zf, zn)
    ext[:, :, 0:2, :] = jnp.zeros_like(ext[:, :, 0:2, :])
    ext[:, :, 2 + ny :, :] = jnp.zeros_like(ext[:, :, 2 + ny :, :])
    ext[:, :, 2 : 2 + ny, 128 : 128 + nz] = own[...].astype(F32)
    ext[:, :, 2 : 2 + ny, 0:128] = zl
    ext[:, :, 2 : 2 + ny, 128 + nz :] = zr
    shift_rows(ext, shifted)
    read = lambda dy, x, p: shifted[dy, x, :, 128 * p : 128 * p + 256]
    pairs = nz // 128 + 1
    size = pairs * 2 * ROWS
    last = nx // 2
    inner = taps(read, [(2 * i, 2 * i + 1) for i in range(last)], pairs)
    low = dot(inner, columns(wa, (0, 1)))
    high = dot(inner, columns(wa, (2, 3)))
    ends[0] = high[:size]
    for i in range(1, last):
        mid[i - 1] = high[i * size : i * size + size] + low[(i - 1) * size : i * size]
    ends[1] = low[(last - 1) * size :]


def side_kernel(place, xf, xn, wa, ends, out, ext, shifted):
    ny = xf.shape[2]
    xl, xr = pick(place[3] == 1, xf, xn)
    ext[:, :, 0:2, :] = jnp.zeros_like(ext[:, :, 0:2, :])
    ext[:, :, 2 + ny :, :] = jnp.zeros_like(ext[:, :, 2 + ny :, :])
    ext[:, 0:2, 2 : 2 + ny, :] = xl
    ext[:, 2:4, 2 : 2 + ny, :] = xr
    shift_rows(ext, shifted)
    read = lambda dy, x, p: shifted[dy, x, :, 128 * p : 128 * p + 256]
    pairs = ext.shape[3] // 128 - 1
    out[0] = ends[0] + dot(taps(read, [(0, 1)], pairs), columns(wa, (0, 1)))
    out[1] = ends[1] + dot(taps(read, [(2, 3)], pairs), columns(wa, (2, 3)))


def silu_pair(pre, direction):
    sig = jax.nn.sigmoid(pre)
    return pre * sig, sig * (1.0 + pre * (1.0 - sig)) * direction


def last_kernel(
    place, yf, yn, mid, ends, wa, wb, bias, out, out_t, edge, acc, hid, shifted
):
    nx, ny, nz = out.shape
    pairs = nz // 128
    yl, yr = pick(place[4] == 1, yf, yn)
    edge[...] = jnp.zeros_like(edge)
    edge[0, :, :, 0:2, :] = yl
    edge[1, :, :, 0:1, :] = yl[:, :, 1:2]
    edge[1, :, :, 3:4, :] = yr[:, :, 0:1]
    edge[2, :, :, 2:4, :] = yr

    def read_edge(dy, x, p):
        part = edge[dy, :, x, :, 128 * p : 128 * p + 256]
        return part.reshape(16, 256).astype(BF16)

    blocks = nx // 2 + 1
    low = taps(read_edge, [(2 * i, 2 * i + 1) for i in range(blocks)], pairs + 1)
    high = taps(read_edge, [(2 * i + 2, 2 * i + 3) for i in range(blocks)], pairs + 1)
    extra = dot(low, columns(wa, (0, 1))) + dot(high, columns(wa, (2, 3)))
    for i in range(blocks):
        if i == 0:
            acc[i] = ends[0]
        elif i == blocks - 1:
            acc[i] = ends[1]
        else:
            acc[i] = mid[i - 1]
        for g in range(2 * (pairs + 1)):
            at = (i * 2 * (pairs + 1) + g) * 8
            top = ROWS * g
            low_end = top + ny
            acc[i, top : top + 2, :] += extra[at : at + 2]
            acc[i, low_end : low_end + 2, :] += extra[at + 2 : at + 4]
    b = bias[0:1, :]
    for i in range(blocks):
        for p in range(pairs + 1):
            at = p * 2 * ROWS
            value = silu_pair(
                acc[i, at : at + ROWS, :] + b, acc[i, at + ROWS : at + 2 * ROWS, :]
            )
            for f in range(2):
                for k in range(2):
                    hid[f, 2 * i + k, 0:ROWS, 128 * p : 128 * p + 128] = value[f][
                        :, 128 * k : 128 * k + 128
                    ]

    def clear(when, index):
        @pl.when(when)
        def _():
            hid[index] = jnp.zeros_like(hid[index])

    every = slice(None)
    clear(place[0] == 0, (every, 0))
    clear(place[0] == place[6] - 1, (every, nx + 1))
    clear(place[1] == 0, (every, every, slice(0, 1)))
    clear(place[1] == place[7] - 1, (every, every, slice(ny + 1, ny + 2)))
    clear(place[2] == 0, (every, every, every, slice(0, 64)))
    clear(place[2] == place[8] - 1, (every, every, every, slice(nz + 64, nz + 128)))

    for dy in range(3):
        for x in range(nx + 2):
            both = jnp.concatenate([hid[f, x, dy : dy + ny, :] for f in range(2)], axis=0)
            shifted[dy, x] = both.astype(BF16)
    read = lambda dy, x, p: shifted[dy, x, :, 128 * p : 128 * p + 256]
    blocks = nx // 2
    low = taps(read, [(2 * i, 2 * i + 1) for i in range(blocks)], pairs)
    high = taps(read, [(2 * i + 2, 2 * i + 3) for i in range(blocks)], pairs)
    total = dot(low, columns(wb, (0, 1))) + dot(high, columns(wb, (2, 3)))
    b = bias[1:2, :]
    for i in range(blocks):
        for p in range(pairs):
            at = (i * pairs + p) * 2 * ny
            value = silu_pair(total[at : at + ny] + b, total[at + ny : at + 2 * ny])
            for target, part in zip((out, out_t), value):
                for k in range(2):
                    target[2 * i + k, :, 128 * p : 128 * p + 128] = part[
                        :, 128 * k : 128 * k + 128
                    ].astype(BF16)


def call(kernel, ins, outs, scratch, args, mib=24):
    return pl.pallas_call(
        kernel,
        in_specs=ins,
        out_specs=[VM] * len(outs),
        out_shape=[jax.ShapeDtypeStruct(*o) for o in outs],
        scratch_shapes=scratch,
        compiler_params=pltpu.CompilerParams(vmem_limit_bytes=mib << 20),
    )(*args)


def shards(source, tangent, first_weight, first_bias, second_weight, second_bias):
    nx, ny, nz = source.shape
    own = lax.optimization_barrier(jnp.stack([source, tangent]))
    names = ("gx", "gy", "gz")
    index = [lax.axis_index(a) for a in names]
    place = jnp.stack(
        [i.astype(jnp.int32) for i in index]
        + [(i % 2 == 0).astype(jnp.int32) for i in index]
        + [jnp.int32(lax.axis_size(a)) for a in names]
    )
    wa, wb, bias = call(
        weight_kernel,
        [HB] * 4,
        [((2304, 128), BF16), ((2304, 128), BF16), ((2, 256), F32)],
        [
            pltpu.VMEM((2, 9, 192, 64), BF16),
            pltpu.VMEM((2, 1, 64), F32),
            pltpu.SemaphoreType.DMA((4,)),
        ],
        (
            first_weight.reshape(9, 192, 64),
            second_weight.reshape(9, 192, 64),
            first_bias.reshape(1, 64),
            second_bias.reshape(1, 64),
        ),
    )
    zf, zn = swap("gz", own[..., :128], own[..., nz - 128 :])
    zl, zr = sides("gz", zf, zn)
    ext = jnp.concatenate([zl, own, zr], axis=3)
    xf, xn = swap("gx", ext[:, :2], ext[:, nx - 2 :])
    xl, xr = sides("gx", xf, xn)
    ends = lambda at: jnp.concatenate(
        [part[:, :, at : at + 2] for part in (xl, ext, xr)], axis=1
    )
    yf, yn = swap("gy", ends(0), ends(ny - 2))

    wide = nz + 256
    blocks = nx // 2 + 1
    size = (nz // 128 + 1) * 2 * ROWS
    work = [
        pltpu.VMEM((2, 4, ROWS + 8, wide), F32),
        pltpu.VMEM((3, 4, 2 * ROWS, wide), BF16),
    ]
    mid, ends_own = call(
        own_kernel,
        [SM] + [VM] * 4,
        [((blocks - 2, size, 256), F32), ((2, size, 256), F32)],
        [
            pltpu.VMEM((2, nx, ROWS + 8, wide), F32),
            pltpu.VMEM((3, nx, 2 * ROWS, wide), BF16),
        ],
        (place, own, zf, zn, wa),
    )
    (outer,) = call(
        side_kernel,
        [SM] + [VM] * 4,
        [((2, size, 256), F32)],
        work,
        (place, xf, xn, wa, ends_own),
    )
    block = ((nx, ny, nz), BF16)
    return tuple(
        call(
            last_kernel,
            [SM] + [VM] * 7,
            [block, block],
            [
                pltpu.VMEM((3, 2, nx + 4, 8, wide), F32),
                pltpu.VMEM((blocks, size, 256), F32),
                pltpu.VMEM((2, nx + 2, ROWS + 8, nz + 128), F32),
                pltpu.VMEM((3, nx + 2, 2 * ny, nz + 128), BF16),
            ],
            (place, yf, yn, mid, outer, wa, wb, bias),
        )
    )


def solution(mesh):
    return jax.shard_map(
        shards,
        mesh=mesh,
        in_specs=(P("gx", "gy", "gz"), P("gx", "gy", "gz"), P(), P(), P(), P()),
        out_specs=(P("gx", "gy", "gz"), P("gx", "gy", "gz")),
        check_vma=False,
    )
```

```python
import functools

import jax
import jax.numpy as jnp
from jax import lax
from jax.experimental import pallas as pl
from jax.experimental.pallas import tpu as pltpu
from jax.sharding import PartitionSpec as P


F32 = jnp.float32
BF16 = jnp.bfloat16
ROWS = 32
VM = pl.BlockSpec(memory_space=pltpu.VMEM)
HB = pl.BlockSpec(memory_space=pltpu.HBM)


def both_ways(pairs):
    return pairs + [(j, i) for i, j in pairs]


def far_pairs(count):
    return [(i, i + 1) for i in range(1, count - 1, 2)]


def near_pairs(count):
    return [(i, i + 1) for i in range(0, count - 1, 2)]


def is_even(axis):
    return lax.axis_index(axis) % 2 == 0


def send(axis, operand, pairs):
    return lax.ppermute(operand, axis, both_ways(pairs))


def swap(axis, head, tail):
    even = is_even(axis)
    count = lax.axis_size(axis)
    far = send(axis, jnp.where(even, head, tail), far_pairs(count))
    near = send(axis, jnp.where(even, tail, head), near_pairs(count))
    return far, near


def sides(axis, far, near):
    even = is_even(axis)
    return jnp.where(even, far, near), jnp.where(even, near, far)


def pick(even, far, near):
    a, b = far[...], near[...]
    return jnp.where(even, a, b).astype(F32), jnp.where(even, b, a).astype(F32)


def late_near(count):
    group = 4
    middle = count // group // 2
    late = []
    for cut in range(group, count - 1, group):
        late.append((cut, cut + 1) if cut <= middle * group else (cut - 2, cut - 1))
    return late


def start_kernel(src, tan, first, second, bias_a, bias_b, own, far, near, raw_a, raw_b, low, sems):
    copies = [
        pltpu.make_async_copy(source, target, sems.at[n])
        for n, (source, target) in enumerate(
            (
                (src, own.at[0]),
                (tan, own.at[1]),
                (first, raw_a),
                (second, raw_b),
                (bias_a, low.at[0]),
                (bias_b, low.at[1]),
            )
        )
    ]
    for copy in copies:
        copy.start()
    even = is_even("gz")
    nz = own.shape[3]
    for f in range(2):
        copies[f].wait()
        head = own[f, :, :, 0:128]
        tail = own[f, :, :, nz - 128 :]
        far[f] = jnp.where(even, head, tail)
        near[f] = jnp.where(even, tail, head)
    for copy in copies[2:]:
        copy.wait()


def weight_kernel(raw_a, raw_b, low, out_a, out_b, bias_out):
    gap = jnp.zeros((64, 64), BF16)
    for raw, target in ((raw_a, out_a), (raw_b, out_b)):
        for tap in range(9):
            w = raw[tap]
            target[256 * tap : 256 * tap + 256, :] = jnp.concatenate(
                [
                    jnp.concatenate([w, gap], axis=0),
                    jnp.concatenate([gap, w], axis=0),
                ],
                axis=1,
            )
    for row in range(2):
        b = low[row]
        bias_out[row : row + 1, :] = jnp.concatenate([b, b, b, b], axis=1)


def columns(weights, planes):
    none = jnp.zeros((256, 128), BF16)

    def tap(dx, dy):
        if not 0 <= dx <= 2:
            return none
        at = 256 * (3 * dx + dy)
        return weights[at : at + 256, :]

    return jnp.concatenate(
        [
            jnp.concatenate([tap(j, dy), tap(j - 1, dy)], axis=1)
            for j in planes
            for dy in range(3)
        ],
        axis=0,
    )


def taps(read, starts, pairs):
    return jnp.concatenate(
        [
            jnp.concatenate(
                [read(dy, x, p) for x in planes for dy in range(3)], axis=1
            )
            for planes in starts
            for p in range(pairs)
        ],
        axis=0,
    )


def dot(lhs, rhs):
    return jnp.dot(lhs, rhs, preferred_element_type=F32)


def shift_rows(ext, shifted):
    for dy in range(3):
        for x in range(shifted.shape[1]):
            both = ext[:, x, dy : dy + ROWS, :].astype(BF16)
            shifted[dy, x] = both.reshape(2 * ROWS, both.shape[2])


def own_kernel(own, zl, zr, wa, mid, ends, ext, shifted):
    nx, ny, nz = own.shape[1:]
    ext[:, :, 0:2, :] = jnp.zeros_like(ext[:, :, 0:2, :])
    ext[:, :, 2 + ny :, :] = jnp.zeros_like(ext[:, :, 2 + ny :, :])
    ext[:, :, 2 : 2 + ny, 128 : 128 + nz] = own[...].astype(F32)
    ext[:, :, 2 : 2 + ny, 0:128] = zl[...].astype(F32)
    ext[:, :, 2 : 2 + ny, 128 + nz :] = zr[...].astype(F32)
    shift_rows(ext, shifted)
    read = lambda dy, x, p: shifted[dy, x, :, 128 * p : 128 * p + 256]
    pairs = nz // 128 + 1
    size = pairs * 2 * ROWS
    last = nx // 2
    inner = taps(read, [(2 * i, 2 * i + 1) for i in range(last)], pairs)
    low = dot(inner, columns(wa, (0, 1)))
    high = dot(inner, columns(wa, (2, 3)))
    ends[0] = high[:size]
    for i in range(1, last):
        mid[i - 1] = high[i * size : i * size + size] + low[(i - 1) * size : i * size]
    ends[1] = low[(last - 1) * size :]


def side_kernel(xl, xr, wa, ends, out, ext, shifted):
    ny = xl.shape[2]
    ext[:, :, 0:2, :] = jnp.zeros_like(ext[:, :, 0:2, :])
    ext[:, :, 2 + ny :, :] = jnp.zeros_like(ext[:, :, 2 + ny :, :])
    ext[:, 0:2, 2 : 2 + ny, :] = xl[...].astype(F32)
    ext[:, 2:4, 2 : 2 + ny, :] = xr[...].astype(F32)
    shift_rows(ext, shifted)
    read = lambda dy, x, p: shifted[dy, x, :, 128 * p : 128 * p + 256]
    pairs = ext.shape[3] // 128 - 1
    out[0] = ends[0] + dot(taps(read, [(0, 1)], pairs), columns(wa, (0, 1)))
    out[1] = ends[1] + dot(taps(read, [(2, 3)], pairs), columns(wa, (2, 3)))


def silu_pair(pre, direction):
    sig = jax.nn.sigmoid(pre)
    return pre * sig, sig * (1.0 + pre * (1.0 - sig)) * direction


def edge_rows(yl, yr, wa, edge, planes, pairs):
    for f in range(2):
        edge[:, 4 * f : 4 * f + 2, :] = yl[f]
        edge[:, 4 * f + 2 : 4 * f + 4, :] = yr[f]
    every = edge[...].reshape(edge.shape[0] * 8, edge.shape[2]).astype(BF16)
    lhs = jnp.concatenate(
        [every[:, 128 * p : 128 * p + 256] for p in range(pairs)], axis=0
    )
    taps_of = lambda dy: [wa[256 * (3 * dx + dy) : 256 * (3 * dx + dy) + 256, :] for dx in range(3)]
    order = taps_of(0) + taps_of(1) + taps_of(2)
    parts = [
        dot(lhs, jnp.concatenate(order[:4], axis=1)),
        dot(lhs, jnp.concatenate(order[4:], axis=1)),
    ]

    def tile(x, p, n):
        at = (p * edge.shape[0] + x) * 8
        part, column = (parts[0], n) if n < 4 else (parts[1], n - 4)
        return part[at : at + 8, 128 * column : 128 * column + 128]

    row = lax.broadcasted_iota(jnp.int32, (8, 128), 0) % 4
    out = {}
    for i in range(planes):
        for p in range(pairs):
            a, b, c = (
                tile(i, p, 3 * dy) + tile(i + 1, p, 3 * dy + 1) + tile(i + 2, p, 3 * dy + 2)
                for dy in range(3)
            )
            above = jnp.where(row == 0, pltpu.roll(b, 7, 0), 0.0)
            below = jnp.where(row == 3, pltpu.roll(b, 1, 0), 0.0)
            out[i, p] = jnp.where(row < 2, a + above, c + below)
    return out


def last_kernel(yf, yn, mid, ends, wa, wb, bias, out, out_t, edge, hid, shifted):
    nx, ny, nz = out.shape
    pairs = nz // 128
    yl, yr = pick(is_even("gy"), yf, yn)
    extra = edge_rows(yl, yr, wa, edge, nx + 2, pairs + 1)

    def limit(axis, low, high):
        at = lax.axis_index(axis)
        return (
            jnp.where(at == 0, low, -1),
            jnp.where(at == lax.axis_size(axis) - 1, high, -1),
        )

    x_low, x_high = limit("gx", 0, nx + 1)
    y_low, y_high = limit("gy", 0, ny + 1)
    z_low, z_high = limit("gz", 0, 1)
    rows = lax.broadcasted_iota(jnp.int32, (ROWS, 128), 0)
    halves = lax.broadcasted_iota(jnp.int32, (ROWS, 128), 1) // 64
    by_row = (rows == y_low) | (rows == y_high)
    first = by_row | (halves == z_low)
    final = by_row | (halves == z_high)
    first_row = lax.broadcasted_iota(jnp.int32, (8, 128), 0) < 2
    b = bias[0:1, 0:128]
    for i in range(nx + 2):
        k = 128 * (i % 2)
        if i < 2:
            source = ends.at[0]
        elif i >= nx:
            source = ends.at[1]
        else:
            source = mid.at[i // 2 - 1]
        for p in range(pairs + 1):
            fields = []
            for f in range(2):
                at = (2 * p + f) * ROWS
                e = extra[i, p]
                up = pltpu.roll(e, 4, 0) if f else e
                fields.append(
                    jnp.concatenate(
                        [
                            source[at : at + 8, k : k + 128] + jnp.where(first_row, up, 0.0),
                            source[at + 8 : at + ny, k : k + 128],
                            source[at + ny : at + ROWS, k : k + 128]
                            + jnp.where(first_row, pltpu.roll(e, 2 if f else 6, 0), 0.0),
                        ],
                        axis=0,
                    )
                )
            outside = first if p == 0 else final if p == pairs else by_row
            if i == 0:
                outside = outside | (rows * 0 == x_low)
            if i == nx + 1:
                outside = outside | (rows * 0 + nx + 1 == x_high)
            for f, value in enumerate(silu_pair(fields[0] + b, fields[1])):
                hid[f, i, 0:ROWS, 128 * p : 128 * p + 128] = jnp.where(outside, 0.0, value)

    for dy in range(3):
        for x in range(nx + 2):
            both = jnp.concatenate([hid[f, x, dy : dy + ny, :] for f in range(2)], axis=0)
            shifted[dy, x] = both.astype(BF16)
    read = lambda dy, x, p: shifted[dy, x, :, 128 * p : 128 * p + 256]
    blocks = nx // 2
    low = taps(read, [(2 * i, 2 * i + 1) for i in range(blocks)], pairs)
    high = taps(read, [(2 * i + 2, 2 * i + 3) for i in range(blocks)], pairs)
    total = dot(low, columns(wb, (0, 1))) + dot(high, columns(wb, (2, 3)))
    b = bias[1:2, :]
    for i in range(blocks):
        for p in range(pairs):
            at = (i * pairs + p) * 2 * ny
            value = silu_pair(total[at : at + ny] + b, total[at + ny : at + 2 * ny])
            for target, part in zip((out, out_t), value):
                for k in range(2):
                    target[2 * i + k, :, 128 * p : 128 * p + 128] = part[
                        :, 128 * k : 128 * k + 128
                    ].astype(BF16)


def call(kernel, ins, outs, scratch, args, mib=24):
    return pl.pallas_call(
        kernel,
        in_specs=ins,
        out_specs=[VM] * len(outs),
        out_shape=[jax.ShapeDtypeStruct(*o) for o in outs],
        scratch_shapes=scratch,
        compiler_params=pltpu.CompilerParams(vmem_limit_bytes=mib << 20),
    )(*args)


def shards(source, tangent, first_weight, first_bias, second_weight, second_bias):
    nx, ny, nz = source.shape
    raw = ((9, 192, 64), BF16)
    tail = ((2, nx, ny, 128), BF16)
    hbm = lambda x: pltpu.with_memory_space_constraint(x, pltpu.HBM)
    own, to_far, to_near, raw_a, raw_b, low = call(
        start_kernel,
        [HB] * 6,
        [((2, nx, ny, nz), BF16), tail, tail, raw, raw, ((2, 1, 64), F32)],
        [pltpu.SemaphoreType.DMA((6,))],
        tuple(
            hbm(x)
            for x in (
                source,
                tangent,
                first_weight.reshape(9, 192, 64),
                second_weight.reshape(9, 192, 64),
                first_bias.reshape(1, 64),
                second_bias.reshape(1, 64),
            )
        ),
    )
    tap = ((2304, 128), BF16)
    wa, wb, bias = call(
        weight_kernel, [VM] * 3, [tap, tap, ((2, 256), F32)], [], (raw_a, raw_b, low)
    )
    count = lax.axis_size("gz")
    late = late_near(count)
    early = [pair for pair in near_pairs(count) if pair not in late]
    z_early = send("gz", to_near, early)
    zf = send("gz", to_far, far_pairs(count))
    z_late = send("gz", to_near, late)
    at = lax.axis_index("gz")
    is_late = functools.reduce(jnp.logical_or, [at // 2 == pair[0] // 2 for pair in late])
    zl, zr = sides("gz", zf, jnp.where(is_late, z_late, z_early))
    ext = jnp.concatenate([zl, own, zr], axis=3)
    xl, xr = sides("gx", *swap("gx", ext[:, :2], ext[:, nx - 2 :]))
    ends = lambda at: jnp.concatenate(
        [part[:, :, at : at + 2] for part in (xl, ext, xr)], axis=1
    )
    yf, yn = swap("gy", ends(0), ends(ny - 2))

    wide = nz + 256
    blocks = nx // 2 + 1
    size = (nz // 128 + 1) * 2 * ROWS
    work = lambda planes: [
        pltpu.VMEM((2, planes, ROWS + 8, wide), F32),
        pltpu.VMEM((3, planes, 2 * ROWS, wide), BF16),
    ]
    mid, ends_own = call(
        own_kernel,
        [VM] * 4,
        [((blocks - 2, size, 256), F32), ((2, size, 256), F32)],
        work(nx),
        (own, zl, zr, wa),
    )
    (outer,) = call(side_kernel, [VM] * 4, [((2, size, 256), F32)], work(4), (xl, xr, wa, ends_own))
    block = ((nx, ny, nz), BF16)
    return tuple(
        call(
            last_kernel,
            [VM] * 7,
            [block, block],
            [
                pltpu.VMEM((nx + 4, 8, wide), F32),
                pltpu.VMEM((2, nx + 2, ROWS + 8, nz + 128), F32),
                pltpu.VMEM((3, nx + 2, 2 * ny, nz + 128), BF16),
            ],
            (yf, yn, mid, outer, wa, wb, bias),
        )
    )


def solution(mesh):
    return jax.shard_map(
        shards,
        mesh=mesh,
        in_specs=(P("gx", "gy", "gz"), P("gx", "gy", "gz"), P(), P(), P(), P()),
        out_specs=(P("gx", "gy", "gz"), P("gx", "gy", "gz")),
        check_vma=False,
    )
```

```python
import jax
import jax.numpy as jnp
from jax import lax
from jax.experimental import pallas as pl
from jax.experimental.pallas import tpu as pltpu
from jax.sharding import PartitionSpec as P


F32 = jnp.float32
BF16 = jnp.bfloat16
ROWS = 32
VM = pl.BlockSpec(memory_space=pltpu.VMEM)
HB = pl.BlockSpec(memory_space=pltpu.HBM)


def both_ways(pairs):
    return pairs + [(j, i) for i, j in pairs]


def far_pairs(count):
    return [(i, i + 1) for i in range(1, count - 1, 2)]


def near_pairs(count):
    return [(i, i + 1) for i in range(0, count - 1, 2)]


def is_even(axis):
    return lax.axis_index(axis) % 2 == 0


def send(axis, operand, pairs):
    return lax.ppermute(operand, axis, both_ways(pairs))


def exchange(axis, to_far, to_near):
    count = lax.axis_size(axis)
    far = send(axis, to_far, far_pairs(count))
    near = send(axis, to_near, near_pairs(count))
    return far, near


def swap(axis, head, tail):
    even = is_even(axis)
    return exchange(axis, jnp.where(even, head, tail), jnp.where(even, tail, head))


def sides(axis, far, near):
    even = is_even(axis)
    return jnp.where(even, far, near), jnp.where(even, near, far)


def pick(even, far, near):
    a, b = far[...], near[...]
    return jnp.where(even, a, b).astype(F32), jnp.where(even, b, a).astype(F32)


def start_kernel(src, tan, far, near, sems):
    even = is_even("gz")
    tail = src.shape[2] - 128
    copies = []
    for f, field in enumerate((src, tan)):
        for n, (target, at) in enumerate(
            ((far, jnp.where(even, 0, tail)), (near, jnp.where(even, tail, 0)))
        ):
            part = field.at[:, :, pl.ds(pl.multiple_of(at, 128), 128)]
            copies.append(pltpu.make_async_copy(part, target.at[f], sems.at[2 * f + n]))
    for copy in copies:
        copy.start()
    for copy in copies:
        copy.wait()


def prep_kernel(
    src, tan, first, second, bias_a, bias_b, own, out_a, out_b, bias_out, raw, low, sems
):
    copies = [
        pltpu.make_async_copy(source, target, sems.at[n])
        for n, (source, target) in enumerate(
            (
                (first, raw.at[0]),
                (second, raw.at[1]),
                (bias_a, low.at[0]),
                (bias_b, low.at[1]),
                (src, own.at[0]),
                (tan, own.at[1]),
            )
        )
    ]
    for copy in copies:
        copy.start()
    gap = jnp.zeros((64, 64), BF16)
    for n, target in enumerate((out_a, out_b)):
        copies[n].wait()
        for tap in range(9):
            w = raw[n, tap]
            target[256 * tap : 256 * tap + 256, :] = jnp.concatenate(
                [
                    jnp.concatenate([w, gap], axis=0),
                    jnp.concatenate([gap, w], axis=0),
                ],
                axis=1,
            )
    for row in range(2):
        copies[2 + row].wait()
        b = low[row]
        bias_out[row : row + 1, :] = jnp.concatenate([b, b, b, b], axis=1)
    for copy in copies[4:]:
        copy.wait()


def columns(weights, planes):
    none = jnp.zeros((256, 128), BF16)

    def tap(dx, dy):
        if not 0 <= dx <= 2:
            return none
        at = 256 * (3 * dx + dy)
        return weights[at : at + 256, :]

    return jnp.concatenate(
        [
            jnp.concatenate([tap(j, dy), tap(j - 1, dy)], axis=1)
            for j in planes
            for dy in range(3)
        ],
        axis=0,
    )


def taps(read, starts, pairs):
    return jnp.concatenate(
        [
            jnp.concatenate(
                [read(dy, x, p) for x in planes for dy in range(3)], axis=1
            )
            for planes in starts
            for p in range(pairs)
        ],
        axis=0,
    )


def dot(lhs, rhs):
    return jnp.dot(lhs, rhs, preferred_element_type=F32)


def shift_rows(ext, shifted):
    for dy in range(3):
        for x in range(shifted.shape[1]):
            both = ext[:, x, dy : dy + ROWS, :].astype(BF16)
            shifted[dy, x] = both.reshape(2 * ROWS, both.shape[2])


def own_kernel(own, zl, zr, wa, mid, ends, ext, shifted):
    nx, ny, nz = own.shape[1:]
    ext[:, :, 0:2, :] = jnp.zeros_like(ext[:, :, 0:2, :])
    ext[:, :, 2 + ny :, :] = jnp.zeros_like(ext[:, :, 2 + ny :, :])
    ext[:, :, 2 : 2 + ny, 128 : 128 + nz] = own[...].astype(F32)
    ext[:, :, 2 : 2 + ny, 0:128] = zl[...].astype(F32)
    ext[:, :, 2 : 2 + ny, 128 + nz :] = zr[...].astype(F32)
    shift_rows(ext, shifted)
    read = lambda dy, x, p: shifted[dy, x, :, 128 * p : 128 * p + 256]
    pairs = nz // 128 + 1
    size = pairs * 2 * ROWS
    last = nx // 2
    inner = taps(read, [(2 * i, 2 * i + 1) for i in range(last)], pairs)
    low = dot(inner, columns(wa, (0, 1)))
    high = dot(inner, columns(wa, (2, 3)))
    ends[0] = high[:size]
    for i in range(1, last):
        mid[i - 1] = high[i * size : i * size + size] + low[(i - 1) * size : i * size]
    ends[1] = low[(last - 1) * size :]


def side_kernel(xl, xr, wa, ends, out, ext, shifted):
    ny = xl.shape[2]
    ext[:, :, 0:2, :] = jnp.zeros_like(ext[:, :, 0:2, :])
    ext[:, :, 2 + ny :, :] = jnp.zeros_like(ext[:, :, 2 + ny :, :])
    ext[:, 0:2, 2 : 2 + ny, :] = xl[...].astype(F32)
    ext[:, 2:4, 2 : 2 + ny, :] = xr[...].astype(F32)
    shift_rows(ext, shifted)
    read = lambda dy, x, p: shifted[dy, x, :, 128 * p : 128 * p + 256]
    pairs = ext.shape[3] // 128 - 1
    out[0] = ends[0] + dot(taps(read, [(0, 1)], pairs), columns(wa, (0, 1)))
    out[1] = ends[1] + dot(taps(read, [(2, 3)], pairs), columns(wa, (2, 3)))


def silu_pair(pre, direction):
    sig = jax.nn.sigmoid(pre)
    return pre * sig, sig * (1.0 + pre * (1.0 - sig)) * direction


def edge_rows(yl, yr, wa, edge, planes, pairs):
    for f in range(2):
        edge[:, 4 * f : 4 * f + 2, :] = yl[f]
        edge[:, 4 * f + 2 : 4 * f + 4, :] = yr[f]
    every = edge[...].reshape(edge.shape[0] * 8, edge.shape[2]).astype(BF16)
    lhs = jnp.concatenate(
        [every[:, 128 * p : 128 * p + 256] for p in range(pairs)], axis=0
    )
    taps_of = lambda dy: [wa[256 * (3 * dx + dy) : 256 * (3 * dx + dy) + 256, :] for dx in range(3)]
    order = taps_of(0) + taps_of(1) + taps_of(2)
    parts = [
        dot(lhs, jnp.concatenate(order[:4], axis=1)),
        dot(lhs, jnp.concatenate(order[4:], axis=1)),
    ]

    def tile(x, p, n):
        at = (p * edge.shape[0] + x) * 8
        part, column = (parts[0], n) if n < 4 else (parts[1], n - 4)
        return part[at : at + 8, 128 * column : 128 * column + 128]

    row = lax.broadcasted_iota(jnp.int32, (8, 128), 0) % 4
    out = {}
    for i in range(planes):
        for p in range(pairs):
            a, b, c = (
                tile(i, p, 3 * dy) + tile(i + 1, p, 3 * dy + 1) + tile(i + 2, p, 3 * dy + 2)
                for dy in range(3)
            )
            above = jnp.where(row == 0, pltpu.roll(b, 7, 0), 0.0)
            below = jnp.where(row == 3, pltpu.roll(b, 1, 0), 0.0)
            out[i, p] = jnp.where(row < 2, a + above, c + below)
    return out


def last_kernel(yf, yn, mid, ends, wa, wb, bias, out, out_t, edge, hid, shifted):
    nx, ny, nz = out.shape
    pairs = nz // 128
    yl, yr = pick(is_even("gy"), yf, yn)
    extra = edge_rows(yl, yr, wa, edge, nx + 2, pairs + 1)

    def limit(axis, low, high):
        at = lax.axis_index(axis)
        return (
            jnp.where(at == 0, low, -1),
            jnp.where(at == lax.axis_size(axis) - 1, high, -1),
        )

    x_low, x_high = limit("gx", 0, nx + 1)
    y_low, y_high = limit("gy", 0, ny + 1)
    z_low, z_high = limit("gz", 0, 1)
    rows = lax.broadcasted_iota(jnp.int32, (ROWS, 128), 0)
    halves = lax.broadcasted_iota(jnp.int32, (ROWS, 128), 1) // 64
    by_row = (rows == y_low) | (rows == y_high)
    first = by_row | (halves == z_low)
    final = by_row | (halves == z_high)
    first_row = lax.broadcasted_iota(jnp.int32, (8, 128), 0) < 2
    b = bias[0:1, 0:128]
    for i in range(nx + 2):
        k = 128 * (i % 2)
        if i < 2:
            source = ends.at[0]
        elif i >= nx:
            source = ends.at[1]
        else:
            source = mid.at[i // 2 - 1]
        for p in range(pairs + 1):
            fields = []
            for f in range(2):
                at = (2 * p + f) * ROWS
                e = extra[i, p]
                up = pltpu.roll(e, 4, 0) if f else e
                fields.append(
                    jnp.concatenate(
                        [
                            source[at : at + 8, k : k + 128] + jnp.where(first_row, up, 0.0),
                            source[at + 8 : at + ny, k : k + 128],
                            source[at + ny : at + ROWS, k : k + 128]
                            + jnp.where(first_row, pltpu.roll(e, 2 if f else 6, 0), 0.0),
                        ],
                        axis=0,
                    )
                )
            outside = first if p == 0 else final if p == pairs else by_row
            if i == 0:
                outside = outside | (rows * 0 == x_low)
            if i == nx + 1:
                outside = outside | (rows * 0 + nx + 1 == x_high)
            for f, value in enumerate(silu_pair(fields[0] + b, fields[1])):
                hid[f, i, 0:ROWS, 128 * p : 128 * p + 128] = jnp.where(outside, 0.0, value)

    for dy in range(3):
        for x in range(nx + 2):
            both = jnp.concatenate([hid[f, x, dy : dy + ny, :] for f in range(2)], axis=0)
            shifted[dy, x] = both.astype(BF16)
    read = lambda dy, x, p: shifted[dy, x, :, 128 * p : 128 * p + 256]
    blocks = nx // 2
    low = taps(read, [(2 * i, 2 * i + 1) for i in range(blocks)], pairs)
    high = taps(read, [(2 * i + 2, 2 * i + 3) for i in range(blocks)], pairs)
    total = dot(low, columns(wb, (0, 1))) + dot(high, columns(wb, (2, 3)))
    b = bias[1:2, :]
    for i in range(blocks):
        for p in range(pairs):
            at = (i * pairs + p) * 2 * ny
            value = silu_pair(total[at : at + ny] + b, total[at + ny : at + 2 * ny])
            for target, part in zip((out, out_t), value):
                for k in range(2):
                    target[2 * i + k, :, 128 * p : 128 * p + 128] = part[
                        :, 128 * k : 128 * k + 128
                    ].astype(BF16)


def call(kernel, ins, outs, scratch, args, mib=24):
    return pl.pallas_call(
        kernel,
        in_specs=ins,
        out_specs=[VM] * len(outs),
        out_shape=[jax.ShapeDtypeStruct(*o) for o in outs],
        scratch_shapes=scratch,
        compiler_params=pltpu.CompilerParams(vmem_limit_bytes=mib << 20),
    )(*args)


def shards(source, tangent, first_weight, first_bias, second_weight, second_bias):
    nx, ny, nz = source.shape
    tail = ((2, nx, ny, 128), BF16)
    hbm = lambda x: pltpu.with_memory_space_constraint(x, pltpu.HBM)
    fields = (hbm(source), hbm(tangent))
    to_far, to_near = call(
        start_kernel, [HB] * 2, [tail, tail], [pltpu.SemaphoreType.DMA((4,))], fields
    )
    tap = ((2304, 128), BF16)
    own, wa, wb, bias = call(
        prep_kernel,
        [HB] * 6,
        [((2, nx, ny, nz), BF16), tap, tap, ((2, 256), F32)],
        [
            pltpu.VMEM((2, 9, 192, 64), BF16),
            pltpu.VMEM((2, 1, 64), F32),
            pltpu.SemaphoreType.DMA((6,)),
        ],
        fields
        + (
            hbm(first_weight.reshape(9, 192, 64)),
            hbm(second_weight.reshape(9, 192, 64)),
            hbm(first_bias.reshape(1, 64)),
            hbm(second_bias.reshape(1, 64)),
        ),
    )
    zl, zr = sides("gz", *exchange("gz", to_far, to_near))
    ext = jnp.concatenate([zl, own, zr], axis=3)
    xl, xr = sides("gx", *swap("gx", ext[:, :2], ext[:, nx - 2 :]))
    ends = lambda at: jnp.concatenate(
        [part[:, :, at : at + 2] for part in (xl, ext, xr)], axis=1
    )
    yf, yn = swap("gy", ends(0), ends(ny - 2))

    wide = nz + 256
    blocks = nx // 2 + 1
    size = (nz // 128 + 1) * 2 * ROWS
    work = lambda planes: [
        pltpu.VMEM((2, planes, ROWS + 8, wide), F32),
        pltpu.VMEM((3, planes, 2 * ROWS, wide), BF16),
    ]
    mid, ends_own = call(
        own_kernel,
        [VM] * 4,
        [((blocks - 2, size, 256), F32), ((2, size, 256), F32)],
        work(nx),
        (own, zl, zr, wa),
    )
    (outer,) = call(side_kernel, [VM] * 4, [((2, size, 256), F32)], work(4), (xl, xr, wa, ends_own))
    block = ((nx, ny, nz), BF16)
    return tuple(
        call(
            last_kernel,
            [VM] * 7,
            [block, block],
            [
                pltpu.VMEM((nx + 4, 8, wide), F32),
                pltpu.VMEM((2, nx + 2, ROWS + 8, nz + 128), F32),
                pltpu.VMEM((3, nx + 2, 2 * ny, nz + 128), BF16),
            ],
            (yf, yn, mid, outer, wa, wb, bias),
        )
    )


def solution(mesh):
    return jax.shard_map(
        shards,
        mesh=mesh,
        in_specs=(P("gx", "gy", "gz"), P("gx", "gy", "gz"), P(), P(), P(), P()),
        out_specs=(P("gx", "gy", "gz"), P("gx", "gy", "gz")),
        check_vma=False,
    )
```

```python
import jax
import jax.numpy as jnp
from jax import lax
from jax.experimental import pallas as pl
from jax.experimental.pallas import tpu as pltpu
from jax.sharding import PartitionSpec as P


F32 = jnp.float32
BF16 = jnp.bfloat16
ROWS = 32
VM = pl.BlockSpec(memory_space=pltpu.VMEM)
HB = pl.BlockSpec(memory_space=pltpu.HBM)


def both_ways(pairs):
    return pairs + [(j, i) for i, j in pairs]


def far_pairs(count):
    return [(i, i + 1) for i in range(1, count - 1, 2)]


def near_pairs(count):
    return [(i, i + 1) for i in range(0, count - 1, 2)]


def is_even(axis):
    return lax.axis_index(axis) % 2 == 0


def send(axis, operand, pairs):
    return lax.ppermute(operand, axis, both_ways(pairs))


def exchange(axis, to_far, to_near):
    count = lax.axis_size(axis)
    far = send(axis, to_far, far_pairs(count))
    near = send(axis, to_near, near_pairs(count))
    return far, near


def swap(axis, head, tail):
    even = is_even(axis)
    return exchange(axis, jnp.where(even, head, tail), jnp.where(even, tail, head))


def sides(axis, far, near):
    even = is_even(axis)
    return jnp.where(even, far, near), jnp.where(even, near, far)


def pick(even, far, near):
    a, b = far[...], near[...]
    return jnp.where(even, a, b).astype(F32), jnp.where(even, b, a).astype(F32)


def start_kernel(src, tan, far, near, sems):
    even = is_even("gz")
    tail = src.shape[2] - 128
    copies = []
    for f, field in enumerate((src, tan)):
        for n, (target, at) in enumerate(
            ((far, jnp.where(even, 0, tail)), (near, jnp.where(even, tail, 0)))
        ):
            part = field.at[:, :, pl.ds(pl.multiple_of(at, 128), 128)]
            copies.append(pltpu.make_async_copy(part, target.at[f], sems.at[2 * f + n]))
    for copy in copies:
        copy.start()
    for copy in copies:
        copy.wait()


def prep_kernel(
    src, tan, first, second, bias_a, bias_b, own, out_a, out_b, bias_out, raw, low, sems
):
    copies = [
        pltpu.make_async_copy(source, target, sems.at[n])
        for n, (source, target) in enumerate(
            (
                (first, raw.at[0]),
                (second, raw.at[1]),
                (bias_a, low.at[0]),
                (bias_b, low.at[1]),
                (src, own.at[0]),
                (tan, own.at[1]),
            )
        )
    ]
    for copy in copies:
        copy.start()
    gap = jnp.zeros((64, 64), BF16)
    for n, target in enumerate((out_a, out_b)):
        copies[n].wait()
        for tap in range(9):
            w = raw[n, tap]
            target[256 * tap : 256 * tap + 256, :] = jnp.concatenate(
                [
                    jnp.concatenate([w, gap], axis=0),
                    jnp.concatenate([gap, w], axis=0),
                ],
                axis=1,
            )
    for row in range(2):
        copies[2 + row].wait()
        b = low[row]
        bias_out[row : row + 1, :] = jnp.concatenate([b, b, b, b], axis=1)
    for copy in copies[4:]:
        copy.wait()


def columns(weights, planes):
    none = jnp.zeros((256, 128), BF16)

    def tap(dx, dy):
        if not 0 <= dx <= 2:
            return none
        at = 256 * (3 * dx + dy)
        return weights[at : at + 256, :]

    return jnp.concatenate(
        [
            jnp.concatenate([tap(j, dy), tap(j - 1, dy)], axis=1)
            for j in planes
            for dy in range(3)
        ],
        axis=0,
    )


def taps(read, starts, pairs):
    return jnp.concatenate(
        [
            jnp.concatenate(
                [read(dy, x, p) for x in planes for dy in range(3)], axis=1
            )
            for planes in starts
            for p in range(pairs)
        ],
        axis=0,
    )


def dot(lhs, rhs):
    return jnp.dot(lhs, rhs, preferred_element_type=F32)


def shift_rows(ext, shifted):
    for dy in range(3):
        for x in range(shifted.shape[1]):
            both = ext[:, x, dy : dy + ROWS, :].astype(BF16)
            shifted[dy, x] = both.reshape(2 * ROWS, both.shape[2])


def own_kernel(own, zl, zr, wa, mid, ends, ext, shifted):
    nx, ny, nz = own.shape[1:]
    ext[:, :, 0:2, :] = jnp.zeros_like(ext[:, :, 0:2, :])
    ext[:, :, 2 + ny :, :] = jnp.zeros_like(ext[:, :, 2 + ny :, :])
    ext[:, :, 2 : 2 + ny, 128 : 128 + nz] = own[...].astype(F32)
    ext[:, :, 2 : 2 + ny, 0:128] = zl[...].astype(F32)
    ext[:, :, 2 : 2 + ny, 128 + nz :] = zr[...].astype(F32)
    shift_rows(ext, shifted)
    read = lambda dy, x, p: shifted[dy, x, :, 128 * p : 128 * p + 256]
    pairs = nz // 128 + 1
    size = pairs * 2 * ROWS
    last = nx // 2
    inner = taps(read, [(2 * i, 2 * i + 1) for i in range(last)], pairs)
    low = dot(inner, columns(wa, (0, 1)))
    high = dot(inner, columns(wa, (2, 3)))
    ends[0] = high[:size]
    for i in range(1, last):
        mid[i - 1] = high[i * size : i * size + size] + low[(i - 1) * size : i * size]
    ends[1] = low[(last - 1) * size :]


def silu_pair(pre, direction):
    sig = jax.nn.sigmoid(pre)
    return pre * sig, sig * (1.0 + pre * (1.0 - sig)) * direction


def limit(axis, low, high):
    at = lax.axis_index(axis)
    return (
        jnp.where(at == 0, low, -1),
        jnp.where(at == lax.axis_size(axis) - 1, high, -1),
    )


def outside_grid(rows, base, planes, pairs):
    x_low, x_high = limit("gx", 0, planes - 1)
    z_low, z_high = limit("gz", 0, 1)
    halves = lax.broadcasted_iota(jnp.int32, rows.shape, 1) // 64
    first = base | (halves == z_low)
    final = base | (halves == z_high)

    def at(i, p):
        drop = first if p == 0 else final if p == pairs - 1 else base
        if i == 0:
            drop = drop | (rows * 0 == x_low)
        if i == planes - 1:
            drop = drop | (rows * 0 + planes - 1 == x_high)
        return drop

    return at


def main_kernel(
    xl, xr, wa, wb, bias, mid, ends, partial, total, ext, shifted, hid, again
):
    ny = xl.shape[2]
    ext[:, :, 0:2, :] = jnp.zeros_like(ext[:, :, 0:2, :])
    ext[:, :, 2 + ny :, :] = jnp.zeros_like(ext[:, :, 2 + ny :, :])
    ext[:, 0:2, 2 : 2 + ny, :] = xl[...].astype(F32)
    ext[:, 2:4, 2 : 2 + ny, :] = xr[...].astype(F32)
    shift_rows(ext, shifted)
    read = lambda dy, x, p: shifted[dy, x, :, 128 * p : 128 * p + 256]
    pairs = ext.shape[3] // 128 - 1
    planes = hid.shape[1]
    left = ends[0] + dot(taps(read, [(0, 1)], pairs), columns(wa, (0, 1)))
    right = ends[1] + dot(taps(read, [(2, 3)], pairs), columns(wa, (2, 3)))

    rows = lax.broadcasted_iota(jnp.int32, (ROWS, 128), 0)
    drop = outside_grid(rows, (rows < 2) | (rows >= ny), planes, pairs)
    b = bias[0:1, 0:128]
    for i in range(planes):
        k = 128 * (i % 2)
        for p in range(pairs):
            fields = []
            for f in range(2):
                at = slice((2 * p + f) * ROWS, (2 * p + f + 1) * ROWS)
                if i < 2:
                    value = left[at, k : k + 128]
                elif i >= planes - 2:
                    value = right[at, k : k + 128]
                else:
                    value = mid[i // 2 - 1, at, k : k + 128]
                lane = slice(128 * p, 128 * p + 128)
                partial[i, 4 * f : 4 * f + 2, lane] = value[0:2]
                partial[i, 4 * f + 2 : 4 * f + 4, lane] = value[ny : ny + 2]
                fields.append(value)
            for f, value in enumerate(silu_pair(fields[0] + b, fields[1])):
                hid[f, i, 0:ROWS, 128 * p : 128 * p + 128] = jnp.where(
                    drop(i, p), 0.0, value
                )

    for dy in range(3):
        for x in range(planes):
            both = jnp.concatenate([hid[f, x, dy : dy + ny, :] for f in range(2)], axis=0)
            again[dy, x] = both.astype(BF16)
    read = lambda dy, x, p: again[dy, x, :, 128 * p : 128 * p + 256]
    blocks = total.shape[0]
    size = total.shape[1]
    low = taps(read, [(2 * i, 2 * i + 1) for i in range(blocks)], pairs - 1)
    high = taps(read, [(2 * i + 2, 2 * i + 3) for i in range(blocks)], pairs - 1)
    result = dot(low, columns(wb, (0, 1))) + dot(high, columns(wb, (2, 3)))
    for i in range(blocks):
        total[i] = result[i * size : i * size + size]


def edge_rows(edge, weights, planes, pairs):
    every = edge[...].reshape(edge.shape[0] * 8, edge.shape[2]).astype(BF16)
    lhs = jnp.concatenate(
        [every[:, 128 * p : 128 * p + 256] for p in range(pairs)], axis=0
    )
    order = [
        weights[256 * (3 * dx + dy) : 256 * (3 * dx + dy) + 256, :]
        for dy in range(3)
        for dx in range(3)
    ]
    parts = [
        dot(lhs, jnp.concatenate(order[:4], axis=1)),
        dot(lhs, jnp.concatenate(order[4:], axis=1)),
    ]

    def tile(x, p, n):
        at = (p * edge.shape[0] + x) * 8
        part, column = (parts[0], n) if n < 4 else (parts[1], n - 4)
        return part[at : at + 8, 128 * column : 128 * column + 128]

    row = lax.broadcasted_iota(jnp.int32, (8, 128), 0) % 4
    out = {}
    for i in range(planes):
        for p in range(pairs):
            a, b, c = (
                tile(i, p, 3 * dy) + tile(i + 1, p, 3 * dy + 1) + tile(i + 2, p, 3 * dy + 2)
                for dy in range(3)
            )
            above = jnp.where(row == 0, pltpu.roll(b, 7, 0), 0.0)
            below = jnp.where(row == 3, pltpu.roll(b, 1, 0), 0.0)
            out[i, p] = jnp.where(row < 2, a + above, c + below)
    return out


def last_kernel(yf, yn, partial, total, wa, wb, bias, out, out_t, edge, edge_hid):
    nx, ny, nz = out.shape
    pairs = nz // 128
    yl, yr = pick(is_even("gy"), yf, yn)
    for f in range(2):
        edge[:, 4 * f : 4 * f + 2, :] = yl[f]
        edge[:, 4 * f + 2 : 4 * f + 4, :] = yr[f]
    extra = edge_rows(edge, wa, nx + 2, pairs + 1)
    row = lax.broadcasted_iota(jnp.int32, (8, 128), 0)
    y_low, y_high = limit("gy", 0, 3)
    drop = outside_grid(
        row, (row % 4 == y_low) | (row % 4 == y_high), nx + 2, pairs + 1
    )
    b = bias[0:1, 0:128]
    for i in range(nx + 2):
        for p in range(pairs + 1):
            lane = slice(128 * p, 128 * p + 128)
            both = extra[i, p] + partial[i, :, lane]
            h, ht = silu_pair(both + b, pltpu.roll(both, 4, 0))
            value = jnp.where(row < 4, h, pltpu.roll(ht, 4, 0))
            edge_hid[i, :, lane] = jnp.where(drop(i, p), 0.0, value)
    extra = edge_rows(edge_hid, wb, nx, pairs)
    b = bias[1:2, 0:128]
    for i in range(nx):
        k = 128 * (i % 2)
        for p in range(pairs):
            near = extra[i, p]
            far = pltpu.roll(near, 4, 0)
            fields = []
            for f in range(2):
                at = (2 * p + f) * ny
                value = total[i // 2, at : at + ny, k : k + 128]
                top, bottom = (near, far) if f == 0 else (far, near)
                fields.append(
                    jnp.concatenate(
                        [
                            value[0:8] + jnp.where(row < 2, top, 0.0),
                            value[8 : ny - 8],
                            value[ny - 8 :] + jnp.where(row >= 6, bottom, 0.0),
                        ],
                        axis=0,
                    )
                )
            for target, value in zip((out, out_t), silu_pair(fields[0] + b, fields[1])):
                target[i, :, 128 * p : 128 * p + 128] = value.astype(BF16)


def call(kernel, ins, outs, scratch, args, mib=24):
    return pl.pallas_call(
        kernel,
        in_specs=ins,
        out_specs=[VM] * len(outs),
        out_shape=[jax.ShapeDtypeStruct(*o) for o in outs],
        scratch_shapes=scratch,
        compiler_params=pltpu.CompilerParams(vmem_limit_bytes=mib << 20),
    )(*args)


def shards(source, tangent, first_weight, first_bias, second_weight, second_bias):
    nx, ny, nz = source.shape
    tail = ((2, nx, ny, 128), BF16)
    hbm = lambda x: pltpu.with_memory_space_constraint(x, pltpu.HBM)
    fields = (hbm(source), hbm(tangent))
    to_far, to_near = call(
        start_kernel, [HB] * 2, [tail, tail], [pltpu.SemaphoreType.DMA((4,))], fields
    )
    tap = ((2304, 128), BF16)
    own, wa, wb, bias = call(
        prep_kernel,
        [HB] * 6,
        [((2, nx, ny, nz), BF16), tap, tap, ((2, 256), F32)],
        [
            pltpu.VMEM((2, 9, 192, 64), BF16),
            pltpu.VMEM((2, 1, 64), F32),
            pltpu.SemaphoreType.DMA((6,)),
        ],
        fields
        + (
            hbm(first_weight.reshape(9, 192, 64)),
            hbm(second_weight.reshape(9, 192, 64)),
            hbm(first_bias.reshape(1, 64)),
            hbm(second_bias.reshape(1, 64)),
        ),
    )
    zl, zr = sides("gz", *exchange("gz", to_far, to_near))
    ext = jnp.concatenate([zl, own, zr], axis=3)
    xl, xr = sides("gx", *swap("gx", ext[:, :2], ext[:, nx - 2 :]))
    ends = lambda at: jnp.concatenate(
        [part[:, :, at : at + 2] for part in (xl, ext, xr)], axis=1
    )
    yf, yn = swap("gy", ends(0), ends(ny - 2))

    wide = nz + 256
    blocks = nx // 2 + 1
    size = (nz // 128 + 1) * 2 * ROWS
    work = lambda planes: [
        pltpu.VMEM((2, planes, ROWS + 8, wide), F32),
        pltpu.VMEM((3, planes, 2 * ROWS, wide), BF16),
    ]
    mid, ends_own = call(
        own_kernel,
        [VM] * 4,
        [((blocks - 2, size, 256), F32), ((2, size, 256), F32)],
        work(nx),
        (own, zl, zr, wa),
    )
    partial, total = call(
        main_kernel,
        [VM] * 7,
        [
            ((nx + 2, 8, nz + 128), F32),
            ((nx // 2, (nz // 128) * 2 * ny, 256), F32),
        ],
        work(4)
        + [
            pltpu.VMEM((2, nx + 2, ROWS + 8, nz + 128), F32),
            pltpu.VMEM((3, nx + 2, 2 * ny, nz + 128), BF16),
        ],
        (xl, xr, wa, wb, bias, mid, ends_own),
    )
    block = ((nx, ny, nz), BF16)
    return tuple(
        call(
            last_kernel,
            [VM] * 7,
            [block, block],
            [
                pltpu.VMEM((nx + 4, 8, wide), F32),
                pltpu.VMEM((nx + 2, 8, nz + 128), F32),
            ],
            (yf, yn, partial, total, wa, wb, bias),
        )
    )


def solution(mesh):
    return jax.shard_map(
        shards,
        mesh=mesh,
        in_specs=(P("gx", "gy", "gz"), P("gx", "gy", "gz"), P(), P(), P(), P()),
        out_specs=(P("gx", "gy", "gz"), P("gx", "gy", "gz")),
        check_vma=False,
    )
```

```python
import jax
import jax.numpy as jnp
from jax import lax
from jax.experimental import pallas as pl
from jax.experimental.pallas import tpu as pltpu
from jax.sharding import PartitionSpec as P


F32 = jnp.float32
BF16 = jnp.bfloat16
ROWS = 32
VM = pl.BlockSpec(memory_space=pltpu.VMEM)
HB = pl.BlockSpec(memory_space=pltpu.HBM)


def both_ways(pairs):
    return pairs + [(j, i) for i, j in pairs]


def far_pairs(count):
    return [(i, i + 1) for i in range(1, count - 1, 2)]


def near_pairs(count):
    return [(i, i + 1) for i in range(0, count - 1, 2)]


FAR_FIRST = {"gx": (True, True), "gy": (True, False), "gz": (True, False)}


def leads_left(axis):
    even, odd = FAR_FIRST[axis]
    far_first = jnp.where(lax.axis_index("gx") % 2 == 0, int(even), int(odd))
    return lax.axis_index(axis) % 2 != far_first


def exchange(axis, first, second):
    count = lax.axis_size(axis)
    kinds = (near_pairs(count), far_pairs(count))
    got = []
    for slot, operand in enumerate((first, second)):
        if axis == "gx":
            over, pairs = axis, kinds[FAR_FIRST[axis][0] ^ (slot == 1)]
        else:
            over, pairs = ("gx", axis), []
            for g in range(lax.axis_size("gx")):
                kind = kinds[FAR_FIRST[axis][g % 2] ^ (slot == 1)]
                pairs += [(g * count + i, g * count + j) for i, j in kind]
        got.append(lax.ppermute(operand, over, both_ways(pairs)))
    return got


def swap(axis, head, tail):
    left = leads_left(axis)
    return exchange(axis, jnp.where(left, head, tail), jnp.where(left, tail, head))


def sides(axis, first, second):
    left = leads_left(axis)
    return jnp.where(left, first, second), jnp.where(left, second, first)


def start_kernel(src, tan, first, second, sems):
    left = leads_left("gz")
    tail = src.shape[2] - 128
    copies = []
    for f, field in enumerate((src, tan)):
        for n, (target, at) in enumerate(
            ((first, jnp.where(left, 0, tail)), (second, jnp.where(left, tail, 0)))
        ):
            part = field.at[:, :, pl.ds(pl.multiple_of(at, 128), 128)]
            copies.append(pltpu.make_async_copy(part, target.at[f], sems.at[2 * f + n]))
    for copy in copies:
        copy.start()
    for copy in copies:
        copy.wait()


def prep_kernel(
    src, tan, first, second, bias_a, bias_b, own, out_a, out_b, bias_out, raw, low, sems
):
    copies = [
        pltpu.make_async_copy(source, target, sems.at[n])
        for n, (source, target) in enumerate(
            (
                (first, raw.at[0]),
                (second, raw.at[1]),
                (bias_a, low.at[0]),
                (bias_b, low.at[1]),
                (src, own.at[0]),
                (tan, own.at[1]),
            )
        )
    ]
    for copy in copies:
        copy.start()
    gap = jnp.zeros((64, 64), BF16)
    for n, target in enumerate((out_a, out_b)):
        copies[n].wait()
        for tap in range(9):
            w = raw[n, tap]
            target[256 * tap : 256 * tap + 256, :] = jnp.concatenate(
                [
                    jnp.concatenate([w, gap], axis=0),
                    jnp.concatenate([gap, w], axis=0),
                ],
                axis=1,
            )
    for row in range(2):
        copies[2 + row].wait()
        b = low[row]
        bias_out[row : row + 1, :] = jnp.concatenate([b, b, b, b], axis=1)
    for copy in copies[4:]:
        copy.wait()


def columns(weights, planes):
    none = jnp.zeros((256, 128), BF16)

    def tap(dx, dy):
        if not 0 <= dx <= 2:
            return none
        at = 256 * (3 * dx + dy)
        return weights[at : at + 256, :]

    return jnp.concatenate(
        [
            jnp.concatenate([tap(j, dy), tap(j - 1, dy)], axis=1)
            for j in planes
            for dy in range(3)
        ],
        axis=0,
    )


def taps(read, starts, pairs):
    return jnp.concatenate(
        [
            jnp.concatenate(
                [read(dy, x, p) for x in planes for dy in range(3)], axis=1
            )
            for planes in starts
            for p in range(pairs)
        ],
        axis=0,
    )


def dot(lhs, rhs):
    return jnp.dot(lhs, rhs, preferred_element_type=F32)


def shift_rows(ext, shifted):
    for dy in range(3):
        for x in range(shifted.shape[1]):
            both = ext[:, x, dy : dy + ROWS, :].astype(BF16)
            shifted[dy, x] = both.reshape(2 * ROWS, both.shape[2])


def own_kernel(own, zl, zr, wa, mid, ends, ext, shifted):
    nx, ny, nz = own.shape[1:]
    ext[:, :, 0:2, :] = jnp.zeros_like(ext[:, :, 0:2, :])
    ext[:, :, 2 + ny :, :] = jnp.zeros_like(ext[:, :, 2 + ny :, :])
    ext[:, :, 2 : 2 + ny, 128 : 128 + nz] = own[...].astype(F32)
    ext[:, :, 2 : 2 + ny, 0:128] = zl[...].astype(F32)
    ext[:, :, 2 : 2 + ny, 128 + nz :] = zr[...].astype(F32)
    shift_rows(ext, shifted)
    read = lambda dy, x, p: shifted[dy, x, :, 128 * p : 128 * p + 256]
    pairs = nz // 128 + 1
    size = pairs * 2 * ROWS
    last = nx // 2
    inner = taps(read, [(2 * i, 2 * i + 1) for i in range(last)], pairs)
    low = dot(inner, columns(wa, (0, 1)))
    high = dot(inner, columns(wa, (2, 3)))
    ends[0] = high[:size]
    for i in range(1, last):
        mid[i - 1] = high[i * size : i * size + size] + low[(i - 1) * size : i * size]
    ends[1] = low[(last - 1) * size :]


def silu_pair(pre, direction):
    sig = jax.nn.sigmoid(pre)
    return pre * sig, sig * (1.0 + pre * (1.0 - sig)) * direction


def limit(axis, low, high):
    at = lax.axis_index(axis)
    return (
        jnp.where(at == 0, low, -1),
        jnp.where(at == lax.axis_size(axis) - 1, high, -1),
    )


def outside_grid(rows, base, planes, pairs):
    x_low, x_high = limit("gx", 0, planes - 1)
    z_low, z_high = limit("gz", 0, 1)
    halves = lax.broadcasted_iota(jnp.int32, rows.shape, 1) // 64
    first = base | (halves == z_low)
    final = base | (halves == z_high)

    def at(i, p):
        drop = first if p == 0 else final if p == pairs - 1 else base
        if i == 0:
            drop = drop | (rows * 0 == x_low)
        if i == planes - 1:
            drop = drop | (rows * 0 + planes - 1 == x_high)
        return drop

    return at


def main_kernel(
    xl, xr, wa, wb, bias, mid, ends, partial, total, ext, shifted, hid, again
):
    ny = xl.shape[2]
    ext[:, :, 0:2, :] = jnp.zeros_like(ext[:, :, 0:2, :])
    ext[:, :, 2 + ny :, :] = jnp.zeros_like(ext[:, :, 2 + ny :, :])
    ext[:, 0:2, 2 : 2 + ny, :] = xl[...].astype(F32)
    ext[:, 2:4, 2 : 2 + ny, :] = xr[...].astype(F32)
    shift_rows(ext, shifted)
    read = lambda dy, x, p: shifted[dy, x, :, 128 * p : 128 * p + 256]
    pairs = ext.shape[3] // 128 - 1
    planes = hid.shape[1]
    left = ends[0] + dot(taps(read, [(0, 1)], pairs), columns(wa, (0, 1)))
    right = ends[1] + dot(taps(read, [(2, 3)], pairs), columns(wa, (2, 3)))

    rows = lax.broadcasted_iota(jnp.int32, (ROWS, 128), 0)
    drop = outside_grid(rows, (rows < 2) | (rows >= ny), planes, pairs)
    b = bias[0:1, 0:128]
    for i in range(planes):
        k = 128 * (i % 2)
        for p in range(pairs):
            fields = []
            for f in range(2):
                at = slice((2 * p + f) * ROWS, (2 * p + f + 1) * ROWS)
                if i < 2:
                    value = left[at, k : k + 128]
                elif i >= planes - 2:
                    value = right[at, k : k + 128]
                else:
                    value = mid[i // 2 - 1, at, k : k + 128]
                lane = slice(128 * p, 128 * p + 128)
                partial[i, 4 * f : 4 * f + 2, lane] = value[0:2]
                partial[i, 4 * f + 2 : 4 * f + 4, lane] = value[ny : ny + 2]
                fields.append(value)
            for f, value in enumerate(silu_pair(fields[0] + b, fields[1])):
                hid[f, i, 0:ROWS, 128 * p : 128 * p + 128] = jnp.where(
                    drop(i, p), 0.0, value
                )

    for dy in range(3):
        for x in range(planes):
            both = jnp.concatenate([hid[f, x, dy : dy + ny, :] for f in range(2)], axis=0)
            again[dy, x] = both.astype(BF16)
    read = lambda dy, x, p: again[dy, x, :, 128 * p : 128 * p + 256]
    blocks = total.shape[0]
    size = total.shape[1]
    low = taps(read, [(2 * i, 2 * i + 1) for i in range(blocks)], pairs - 1)
    high = taps(read, [(2 * i + 2, 2 * i + 3) for i in range(blocks)], pairs - 1)
    result = dot(low, columns(wb, (0, 1))) + dot(high, columns(wb, (2, 3)))
    for i in range(blocks):
        total[i] = result[i * size : i * size + size]


def edge_rows(edge, weights, planes, pairs):
    every = edge[...].reshape(edge.shape[0] * 8, edge.shape[2]).astype(BF16)
    lhs = jnp.concatenate(
        [every[:, 128 * p : 128 * p + 256] for p in range(pairs)], axis=0
    )
    order = [
        weights[256 * (3 * dx + dy) : 256 * (3 * dx + dy) + 256, :]
        for dy in range(3)
        for dx in range(3)
    ]
    parts = [
        dot(lhs, jnp.concatenate(order[:4], axis=1)),
        dot(lhs, jnp.concatenate(order[4:], axis=1)),
    ]

    def tile(x, p, n):
        at = (p * edge.shape[0] + x) * 8
        part, column = (parts[0], n) if n < 4 else (parts[1], n - 4)
        return part[at : at + 8, 128 * column : 128 * column + 128]

    row = lax.broadcasted_iota(jnp.int32, (8, 128), 0) % 4
    out = {}
    for i in range(planes):
        for p in range(pairs):
            a, b, c = (
                tile(i, p, 3 * dy) + tile(i + 1, p, 3 * dy + 1) + tile(i + 2, p, 3 * dy + 2)
                for dy in range(3)
            )
            above = jnp.where(row == 0, pltpu.roll(b, 7, 0), 0.0)
            below = jnp.where(row == 3, pltpu.roll(b, 1, 0), 0.0)
            out[i, p] = jnp.where(row < 2, a + above, c + below)
    return out


def last_kernel(first, second, partial, total, wa, wb, bias, out, out_t, edge, edge_hid):
    nx, ny, nz = out.shape
    pairs = nz // 128
    left = leads_left("gy")
    one, two = first[...].astype(F32), second[...].astype(F32)
    yl = jnp.where(left, one, two)
    yr = jnp.where(left, two, one)
    for f in range(2):
        edge[:, 4 * f : 4 * f + 2, :] = yl[f]
        edge[:, 4 * f + 2 : 4 * f + 4, :] = yr[f]
    extra = edge_rows(edge, wa, nx + 2, pairs + 1)
    row = lax.broadcasted_iota(jnp.int32, (8, 128), 0)
    y_low, y_high = limit("gy", 0, 3)
    drop = outside_grid(
        row, (row % 4 == y_low) | (row % 4 == y_high), nx + 2, pairs + 1
    )
    b = bias[0:1, 0:128]
    for i in range(nx + 2):
        for p in range(pairs + 1):
            lane = slice(128 * p, 128 * p + 128)
            both = extra[i, p] + partial[i, :, lane]
            h, ht = silu_pair(both + b, pltpu.roll(both, 4, 0))
            value = jnp.where(row < 4, h, pltpu.roll(ht, 4, 0))
            edge_hid[i, :, lane] = jnp.where(drop(i, p), 0.0, value)
    extra = edge_rows(edge_hid, wb, nx, pairs)
    b = bias[1:2, 0:128]
    for i in range(nx):
        k = 128 * (i % 2)
        for p in range(pairs):
            near = extra[i, p]
            far = pltpu.roll(near, 4, 0)
            fields = []
            for f in range(2):
                at = (2 * p + f) * ny
                value = total[i // 2, at : at + ny, k : k + 128]
                top, bottom = (near, far) if f == 0 else (far, near)
                fields.append(
                    jnp.concatenate(
                        [
                            value[0:8] + jnp.where(row < 2, top, 0.0),
                            value[8 : ny - 8],
                            value[ny - 8 :] + jnp.where(row >= 6, bottom, 0.0),
                        ],
                        axis=0,
                    )
                )
            for target, value in zip((out, out_t), silu_pair(fields[0] + b, fields[1])):
                target[i, :, 128 * p : 128 * p + 128] = value.astype(BF16)


def call(kernel, ins, outs, scratch, args, mib=24):
    return pl.pallas_call(
        kernel,
        in_specs=ins,
        out_specs=[VM] * len(outs),
        out_shape=[jax.ShapeDtypeStruct(*o) for o in outs],
        scratch_shapes=scratch,
        compiler_params=pltpu.CompilerParams(vmem_limit_bytes=mib << 20),
    )(*args)


def shards(source, tangent, first_weight, first_bias, second_weight, second_bias):
    nx, ny, nz = source.shape
    tail = ((2, nx, ny, 128), BF16)
    hbm = lambda x: pltpu.with_memory_space_constraint(x, pltpu.HBM)
    fields = (hbm(source), hbm(tangent))
    ends_first, ends_second = call(
        start_kernel, [HB] * 2, [tail, tail], [pltpu.SemaphoreType.DMA((4,))], fields
    )
    tap = ((2304, 128), BF16)
    own, wa, wb, bias = call(
        prep_kernel,
        [HB] * 6,
        [((2, nx, ny, nz), BF16), tap, tap, ((2, 256), F32)],
        [
            pltpu.VMEM((2, 9, 192, 64), BF16),
            pltpu.VMEM((2, 1, 64), F32),
            pltpu.SemaphoreType.DMA((6,)),
        ],
        fields
        + (
            hbm(first_weight.reshape(9, 192, 64)),
            hbm(second_weight.reshape(9, 192, 64)),
            hbm(first_bias.reshape(1, 64)),
            hbm(second_bias.reshape(1, 64)),
        ),
    )
    zl, zr = sides("gz", *exchange("gz", ends_first, ends_second))
    ext = jnp.concatenate([zl, own, zr], axis=3)
    xl, xr = sides("gx", *swap("gx", ext[:, :2], ext[:, nx - 2 :]))
    ends = lambda at: jnp.concatenate(
        [part[:, :, at : at + 2] for part in (xl, ext, xr)], axis=1
    )
    y_first, y_second = swap("gy", ends(0), ends(ny - 2))

    wide = nz + 256
    blocks = nx // 2 + 1
    size = (nz // 128 + 1) * 2 * ROWS
    work = lambda planes: [
        pltpu.VMEM((2, planes, ROWS + 8, wide), F32),
        pltpu.VMEM((3, planes, 2 * ROWS, wide), BF16),
    ]
    mid, ends_own = call(
        own_kernel,
        [VM] * 4,
        [((blocks - 2, size, 256), F32), ((2, size, 256), F32)],
        work(nx),
        (own, zl, zr, wa),
    )
    partial, total = call(
        main_kernel,
        [VM] * 7,
        [
            ((nx + 2, 8, nz + 128), F32),
            ((nx // 2, (nz // 128) * 2 * ny, 256), F32),
        ],
        work(4)
        + [
            pltpu.VMEM((2, nx + 2, ROWS + 8, nz + 128), F32),
            pltpu.VMEM((3, nx + 2, 2 * ny, nz + 128), BF16),
        ],
        (xl, xr, wa, wb, bias, mid, ends_own),
    )
    block = ((nx, ny, nz), BF16)
    return tuple(
        call(
            last_kernel,
            [VM] * 7,
            [block, block],
            [
                pltpu.VMEM((nx + 4, 8, wide), F32),
                pltpu.VMEM((nx + 2, 8, nz + 128), F32),
            ],
            (y_first, y_second, partial, total, wa, wb, bias),
        )
    )


def solution(mesh):
    return jax.shard_map(
        shards,
        mesh=mesh,
        in_specs=(P("gx", "gy", "gz"), P("gx", "gy", "gz"), P(), P(), P(), P()),
        out_specs=(P("gx", "gy", "gz"), P("gx", "gy", "gz")),
        check_vma=False,
    )
```
